32 devices in a mesh: gx: 4 (over y, x), gy: 4 (over z), gz: 2 (over core).
Axes of the slice: x: 2, y: 2, z: 4, core: 2. Of those that a mesh axis runs over, the one named last changes fastest.
Arguments:
- checkpoint: float32 [19, 8, 64, 256], P(None, 'gx', 'gy', 'gz'), may hold values from 0 to 1, as said below
- resistance: float32 [8, 64, 256], P('gx', 'gy', 'gz'), may hold values from 0.01 to 1
- solid: int32 [8, 64, 256], P('gx', 'gy', 'gz'), may hold values 0 or 1
- adjoint_final: float32 [19, 8, 64, 256], P(None, 'gx', 'gy', 'gz'), may hold values from -6 to 6
Outputs:
- adjoint_start: float32 [19, 8, 64, 256], P(None, 'gx', 'gy', 'gz')
- sensitivity: float32 [8, 64, 256], P('gx', 'gy', 'gz')
The draws below stay inside these ranges and needn't reach their ends.
Inputs may be any that keep to these rules, and one draw needn't show every extreme that they name: `checkpoint`: every population is positive, near w_i times a density of order one.
All inputs are finite; a program needn't handle non-finite values. No bound on the sum of `solid` on one device may be relied on, other than what follows from the above.
Results may differ from the reference program's by a relative error of at most 0.0003.
Values sent between devices are 32-bit elements; how exact they have to be, the bound alone decides.
No kernel may reach another device: no remote copies, remote signals or barrier semaphores. Data moves between devices by JAX's collectives and lax.ppermute only.
A program may use at most 64 MiB of HBM per device.

```python
import math
import jax
import jax.numpy as jnp
from jax import lax

Q = 19
STEPS = 4
NX = 8
NY = 64
NZ = 256


def draw_checkpoint(key, part):
    table = jnp.array((1.0 / 3.0,) + (1.0 / 18.0,) * 6 + (1.0 / 36.0,) * 12, jnp.float32).reshape(-1, 1, 1, 1)
    factor = jax.random.uniform(key, (Q, NX, NY, NZ), jnp.float32, 0.7, 1.3)
    return table * factor


def with_ends(values, rng, low, largest):
    spot = [jax.random.randint(jax.random.fold_in(rng, axis), (), 0, length) for axis, length in enumerate(values.shape)]
    widest = values.shape.index(max(values.shape))
    next_to = spot[:widest] + [(spot[widest] + 1) % values.shape[widest]] + spot[widest + 1:]
    return values.at[tuple(spot)].set(low).at[tuple(next_to)].set(largest)


def level_of(rng, extent, split, least, top_value):
    loudness, own = 1.0, jax.random.fold_in(rng, 6)
    for axis_at, parts in split:
        heights = jnp.exp(jax.random.uniform(jax.random.fold_in(own, axis_at), (parts,), jnp.float32, least / len(split), top_value / len(split)))
        loudness = loudness * jnp.repeat(heights, extent[axis_at] // parts).reshape([-1 if axis == axis_at else 1 for axis in range(len(extent))])
    return loudness


def bell_draw(stream_key, dims, width, reach, pieces=(), kind=jnp.bfloat16):
    drawn = width * jax.random.normal(stream_key, dims, jnp.float32)
    if pieces:
        drawn = drawn * level_of(stream_key, dims, pieces, -0.22, 0.18)
    return jnp.clip(drawn, -reach, reach).astype(kind)


def setup_inputs(seed: int = 0) -> dict:
    arg_keys = jax.random.split(jax.random.key(seed), 5)
    return {
        "checkpoint": draw_checkpoint(jax.random.fold_in(arg_keys[4], 71), 0),
        "resistance": jnp.clip(jnp.exp(math.log(1.0) - 4.6051702 * jax.random.uniform(arg_keys[1], (NX, NY, NZ), jnp.float32) ** level_of(arg_keys[1], (NX, NY, NZ), ((0, 4), (1, 4), (2, 2)), -0.2, 0.2)), 0.01, 1.0),
        "solid": with_ends((jax.random.randint(arg_keys[2], (NX, NY, NZ), 0, 4) < 1).astype(jnp.int32), jax.random.fold_in(arg_keys[2], 1), 0, 1),
        "adjoint_final": bell_draw(arg_keys[3], (Q, NX, NY, NZ), 1.0, 6.0, ((1, 4), (2, 4), (3, 2)), jnp.float32),
    }


VELOCITIES = ((0, 0, 0), (1, 0, 0), (-1, 0, 0), (0, 1, 0), (0, -1, 0), (0, 0, 1), (0, 0, -1), (1, 1, 0), (-1, -1, 0), (1, -1, 0), (-1, 1, 0), (1, 0, 1), (-1, 0, -1), (1, 0, -1), (-1, 0, 1), (0, 1, 1), (0, -1, -1), (0, 1, -1), (0, -1, 1))
WEIGHTS = (1.0 / 3.0,) + (1.0 / 18.0,) * 6 + (1.0 / 36.0,) * 12
OPPOSITE = tuple((VELOCITIES.index((-entry[0], -entry[1], -entry[2])) for entry in VELOCITIES))
RELAXATION = 0.8
BODY_FORCE = 0.01

def collide(populations, resistance, solid):
    lattice = jnp.array(VELOCITIES, jnp.float32)
    weights = jnp.array(WEIGHTS, jnp.float32).reshape(-1, 1, 1, 1)
    density = lax.optimization_barrier(jnp.sum(populations, axis=0))
    momentum = jnp.tensordot(lattice, populations, axes=([0], [0]), precision=lax.Precision.HIGHEST)
    nothing = jnp.zeros_like(density)
    push = jnp.stack([BODY_FORCE * density, nothing, nothing]) - resistance[None] * momentum
    velocity = (momentum + RELAXATION * push) / density[None]
    projected = jnp.tensordot(lattice, velocity, axes=([1], [0]), precision=lax.Precision.HIGHEST)
    speed_squared = lax.optimization_barrier(jnp.sum(velocity * velocity, axis=0))
    equilibrium = weights * density[None] * (1.0 + 3.0 * projected + 4.5 * projected * projected - 1.5 * speed_squared[None])
    relaxed = populations - (populations - equilibrium) / RELAXATION
    reflected = jnp.stack([populations[other] for other in OPPOSITE])
    return jnp.where(solid[None] == 1, reflected, relaxed)

def stream(collided):
    return jnp.stack([jnp.roll(collided[number], VELOCITIES[number], axis=(0, 1, 2)) for number in range(len(VELOCITIES))])

def reference(checkpoint, resistance, solid, adjoint_final):

    def one_step(populations, design):
        return stream(collide(populations, design, solid))
    guarded = jax.checkpoint(one_step)

    def advance(populations, design):
        for step in range(STEPS):
            populations = guarded(populations, design)
        return populations
    result, pull = jax.vjp(advance, checkpoint, resistance)
    adjoint_start, sensitivity = pull(adjoint_final)
    return (adjoint_start, sensitivity)
```

```python
import functools

import jax
import jax.numpy as jnp
from jax import lax
from jax.experimental import pallas as pl
from jax.experimental.pallas import tpu as pltpu
from jax.sharding import PartitionSpec as P

STEPS = 4


VELOCITIES = (
    (0, 0, 0),
    (1, 0, 0),
    (-1, 0, 0),
    (0, 1, 0),
    (0, -1, 0),
    (0, 0, 1),
    (0, 0, -1),
    (1, 1, 0),
    (-1, -1, 0),
    (1, -1, 0),
    (-1, 1, 0),
    (1, 0, 1),
    (-1, 0, -1),
    (1, 0, -1),
    (-1, 0, 1),
    (0, 1, 1),
    (0, -1, -1),
    (0, 1, -1),
    (0, -1, 1),
)
WEIGHTS = (1.0 / 3.0,) + (1.0 / 18.0,) * 6 + (1.0 / 36.0,) * 12
OPPOSITE = tuple((VELOCITIES.index((-entry[0], -entry[1], -entry[2])) for entry in VELOCITIES))
RELAXATION = 0.8
BODY_FORCE = 0.01

Q = len(VELOCITIES)
KEEP = 1.0 - 1.0 / RELAXATION
PUSH = RELAXATION * BODY_FORCE
VMEM_LIMIT = 16 * 1024 * 1024

GROUP = 4
ROWS = 4
LAYERS = 2
HALO = 3
RES, SOL, ADJ = Q, Q + 1, Q + 2
FIELDS = Q + 2 + Q

FORWARD_UP = (
    [(3, i, -1) for i in range(Q)]
    + [(2, i, -2) for i in range(Q) if VELOCITIES[i][1] >= 0]
    + [(1, i, -3) for i in range(Q) if VELOCITIES[i][1] > 0]
    + [(3, RES, -1), (3, SOL, -1), (2, RES, -2), (2, SOL, -2)]
    + [(3, ADJ + i, -1) for i in range(Q) if VELOCITIES[i][1] < 0]
)
FORWARD_DOWN = (
    [(0, i, 4) for i in range(Q)]
    + [(1, i, 5) for i in range(Q) if VELOCITIES[i][1] <= 0]
    + [(2, i, 6) for i in range(Q) if VELOCITIES[i][1] < 0]
    + [(0, RES, 4), (0, SOL, 4), (1, RES, 5), (1, SOL, 5)]
    + [(0, ADJ + i, 4) for i in range(Q) if VELOCITIES[i][1] > 0]
)
BACKWARD_UP = (
    [(3, i, -1) for i in range(Q)]
    + [(2, i, -2) for i in range(Q) if VELOCITIES[i][1] <= 0]
    + [(1, i, -3) for i in range(Q) if VELOCITIES[i][1] < 0]
    + [(2, Q + j, -2) for j in range(4)]
)
BACKWARD_DOWN = (
    [(0, i, 4) for i in range(Q)]
    + [(1, i, 5) for i in range(Q) if VELOCITIES[i][1] >= 0]
    + [(2, i, 6) for i in range(Q) if VELOCITIES[i][1] > 0]
    + [(1, Q + j, 5) for j in range(4)]
)


def moments(f):
    plus = [f[i] + f[i + 1] for i in range(1, Q, 2)]
    less = [f[i] - f[i + 1] for i in range(1, Q, 2)]
    density = f[0] + ((plus[0] + plus[1]) + (plus[2] + plus[3])) + ((plus[4] + plus[5]) + (plus[6] + (plus[7] + plus[8])))
    first = less[0] + ((less[3] + less[4]) + (less[5] + less[6]))
    second = less[1] + ((less[3] - less[4]) + (less[7] + less[8]))
    third = less[2] + ((less[5] - less[6]) + (less[7] - less[8]))
    inverse = 1.0 / density
    return density, first * inverse, second * inverse, third * inverse


def along(i, x, y, z):
    total = None
    for sign, part in zip(VELOCITIES[i], (x, y, z)):
        if sign == 0:
            continue
        if total is None:
            total = part if sign > 0 else -part
        else:
            total = total + part if sign > 0 else total - part
    return total


def collide_lists(f, density, vx, vy, vz, resistance, solid):
    damp = 1.0 - RELAXATION * resistance
    ux, uy, uz = damp * vx + PUSH, damp * vy, damp * vz
    base = 1.0 - 1.5 * (ux * ux + uy * uy + uz * uz)
    scaled = {w: density * (w / RELAXATION) for w in sorted(set(WEIGHTS))}
    out = [jnp.where(solid, f[0], KEEP * f[0] + scaled[WEIGHTS[0]] * base)]
    for i in range(1, Q, 2):
        projected = along(i, ux, uy, uz)
        weight = scaled[WEIGHTS[i]]
        even = weight * (base + 4.5 * (projected * projected))
        odd = weight * (3.0 * projected)
        out.append(jnp.where(solid, f[i + 1], KEEP * f[i] + (even + odd)))
        out.append(jnp.where(solid, f[i], KEEP * f[i + 1] + (even - odd)))
    return out


def adjoint_lists(mu, density, vx, vy, vz, resistance, solid):
    damp = 1.0 - RELAXATION * resistance
    ux, uy, uz = damp * vx + PUSH, damp * vy, damp * vz
    plus = [mu[i] + mu[i + 1] for i in range(1, Q, 2)]
    less = [mu[i] - mu[i + 1] for i in range(1, Q, 2)]
    rest, axis, diagonal = (w / RELAXATION for w in (WEIGHTS[0], WEIGHTS[1], WEIGHTS[7]))
    xy, xz, yz = plus[3] + plus[4], plus[5] + plus[6], plus[7] + plus[8]
    zeroth = rest * mu[0] + axis * ((plus[0] + plus[1]) + plus[2]) + diagonal * ((xy + xz) + yz)
    nx = axis * less[0] + diagonal * ((less[3] + less[4]) + (less[5] + less[6]))
    ny = axis * less[1] + diagonal * ((less[3] - less[4]) + (less[7] + less[8]))
    nz = axis * less[2] + diagonal * ((less[5] - less[6]) + (less[7] - less[8]))
    nxx = axis * plus[0] + diagonal * (xy + xz)
    nyy = axis * plus[1] + diagonal * (xy + yz)
    nzz = axis * plus[2] + diagonal * (xz + yz)
    nxy = diagonal * (plus[3] - plus[4])
    nxz = diagonal * (plus[5] - plus[6])
    nyz = diagonal * (plus[7] - plus[8])
    tx = nxx * ux + nxy * uy + nxz * uz
    ty = nxy * ux + nyy * uy + nyz * uz
    tz = nxz * ux + nyz * uy + nzz * uz
    hx = 3.0 * (nx - ux * zeroth) + 9.0 * tx
    hy = 3.0 * (ny - uy * zeroth) + 9.0 * ty
    hz = 3.0 * (nz - uz * zeroth) + 9.0 * tz
    pulled = vx * hx + vy * hy + vz * hz
    square = ux * ux + uy * uy + uz * uz
    scalar = (
        zeroth * (1.0 - 1.5 * square)
        + 3.0 * (nx * ux + ny * uy + nz * uz)
        + 4.5 * (tx * ux + ty * uy + tz * uz)
        - damp * pulled
    )
    qx, qy, qz = damp * hx, damp * hy, damp * hz
    out = [jnp.where(solid, mu[0], KEEP * mu[0] + scalar)]
    for i in range(1, Q, 2):
        slope = along(i, qx, qy, qz)
        out.append(jnp.where(solid, mu[i + 1], KEEP * mu[i] + (scalar + slope)))
        out.append(jnp.where(solid, mu[i], KEEP * mu[i + 1] + (scalar - slope)))
    design = jnp.where(solid, 0.0, (-RELAXATION) * density * pulled)
    return out, design


def shifted(value, i, sign):
    first, _, third = VELOCITIES[i]
    if first:
        value = pltpu.roll(value, (sign * first) % value.shape[0], axis=0)
    if third:
        value = pltpu.roll(value, (sign * third) % value.shape[1], axis=1)
    return value


def block_of(number):
    gray = number ^ (number >> 1)
    odd = lax.axis_index("gy") % 2
    return gray + odd * (GROUP - 1 - 2 * gray)


def send_kernel(f_ref, r_ref, s_ref, a_ref, *refs):
    outs, blocks = refs[:GROUP], refs[GROUP]
    for half in range(2):
        rows = pl.ds(8 * half, 8)
        tiles = []
        for layer in range(LAYERS):
            f = [f_ref[i, layer, rows, :] for i in range(Q)]
            resistance, kind = r_ref[layer, rows, :], s_ref[layer, rows, :]
            out = collide_lists(f, *moments(f), resistance, kind == 1)
            out += [resistance, kind.astype(jnp.float32)]
            out += [a_ref[i, layer, rows, :] for i in range(Q)]
            tiles.append(out)
        for field in range(FIELDS):
            first, second = tiles[0][field], tiles[1][field]
            blocks[2 * half, field] = jnp.concatenate([first[:4], second[:4]], axis=0)
            blocks[2 * half + 1, field] = jnp.concatenate([first[4:], second[4:]], axis=0)
    here = lax.axis_index("gx")
    for k in range(GROUP):
        outs[k][...] = blocks[block_of(here ^ k)]


def turn_kernel(*refs):
    ins, (own, up, down, flat) = refs[:GROUP], refs[GROUP:]
    here = lax.axis_index("gx")
    for k in range(GROUP):
        start = 8 * (here ^ k)
        for field in range(FIELDS):
            flat[field, pl.ds(pl.multiple_of(start, 8), 8), :] = ins[k][field]
    for field in range(FIELDS):
        for row in range(ROWS):
            own[row, field] = flat[field, pl.ds(row, 8, stride=ROWS), :]
    for number, (row, field, _) in enumerate(FORWARD_UP):
        up[number] = own[row, field]
    for number, (row, field, _) in enumerate(FORWARD_DOWN):
        down[number] = own[row, field]


def forward_kernel(own_a, own_b, lo_a, lo_b, hi_a, hi_b, lam_ref, sens_ref, mom1, mom2, rs_ref, up, down, p0, p1, p2, a4):
    for side, own, lo, hi in ((0, own_a, lo_a, hi_a), (1, own_b, lo_b, hi_b)):
        lanes = slice(128 * side, 128 * side + 128)
        for row in range(ROWS):
            for i in range(Q):
                p0[row + 3, i, :, lanes] = own[row, i]
                a4[row + 1, i, :, lanes] = own[row, ADJ + i]
            for j in range(2):
                rs_ref[row + 2, j, :, lanes] = own[row, RES + j]
        for table, part in ((FORWARD_UP, lo), (FORWARD_DOWN, hi)):
            for number, (_, field, row) in enumerate(table):
                if field < Q:
                    p0[row + 3, field, :, lanes] = part[number]
                elif field < ADJ:
                    rs_ref[row + 2, field - RES, :, lanes] = part[number]
                else:
                    a4[row + 1, field - ADJ, :, lanes] = part[number]

    def pull(source, row):
        return [shifted(source[row + 1 - VELOCITIES[i][1], i], i, 1) for i in range(Q)]

    def first(row, _):
        f = pull(p0, row)
        moment = moments(f)
        for j in range(4):
            mom1[row, j] = moment[j]
        out = collide_lists(f, *moment, rs_ref[row, 0], rs_ref[row, 1] == 1.0)
        for i in range(Q):
            p1[row, i] = out[i]
        return 0

    lax.fori_loop(0, ROWS + 4, first, 0)

    def second(row, _):
        f = pull(p1, row)
        moment = moments(f)
        for j in range(4):
            mom2[row + 1, j] = moment[j]
        out = collide_lists(f, *moment, rs_ref[row + 1, 0], rs_ref[row + 1, 1] == 1.0)
        for i in range(Q):
            p2[row, i] = out[i]
        return 0

    lax.fori_loop(0, ROWS + 2, second, 0)

    def third(row, _):
        moment = moments(pull(p2, row))
        mu = [shifted(a4[row + 1 + VELOCITIES[i][1], i], i, -1) for i in range(Q)]
        out, design = adjoint_lists(mu, *moment, rs_ref[row + 2, 0], rs_ref[row + 2, 1] == 1.0)
        for i in range(Q):
            lam_ref[row, i] = out[i]
        sens_ref[row] = design[:, :128]
        return 0

    lax.fori_loop(0, ROWS, third, 0)
    for table, part in ((BACKWARD_UP, up), (BACKWARD_DOWN, down)):
        for number, (row, field, _) in enumerate(table):
            source = lam_ref[row, field, :, :128] if field < Q else mom2[row + 2, field - Q, :, :128]
            part[number] = source
    for row in (0, ROWS + 3):
        for j in range(4):
            mom2[row, j] = jnp.zeros((8, 256), jnp.float32)


def backward_kernel(lam_ref, sens_ref, mom1, mom2, rs_ref, lo_a, lo_b, hi_a, hi_b, *refs):
    outs, (l3, l2, l1, m2, flat) = refs[:GROUP], refs[GROUP:]
    for row in range(ROWS):
        for i in range(Q):
            l3[row + 3, i] = lam_ref[row, i]
    for row in range(ROWS + 4):
        for j in range(4):
            m2[row, j] = mom2[row, j]
    for side, lo, hi in ((0, lo_a, hi_a), (1, lo_b, hi_b)):
        lanes = slice(128 * side, 128 * side + 128)
        for table, part in ((BACKWARD_UP, lo), (BACKWARD_DOWN, hi)):
            for number, (_, field, row) in enumerate(table):
                if field < Q:
                    l3[row + 3, field, :, lanes] = part[number]
                else:
                    m2[row + 2, field - Q, :, lanes] = part[number]

    def pull(source, row):
        return [shifted(source[row + 1 + VELOCITIES[i][1], i], i, -1) for i in range(Q)]

    designs = flat.at[Q]

    def second(row, _):
        mu = pull(l3, row)
        out, design = adjoint_lists(mu, *[m2[row, j] for j in range(4)], rs_ref[row, 0], rs_ref[row, 1] == 1.0)
        for i in range(Q):
            l2[row, i] = out[i]
        l1[row, 0] = design
        return 0

    lax.fori_loop(0, ROWS + 4, second, 0)
    total = [sens_ref[row] + l1[row + 2, 0, :, :128] for row in range(ROWS)]

    def first(row, _):
        mu = pull(l2, row)
        out, design = adjoint_lists(
            mu, *[mom1[row + 1, j] for j in range(4)], rs_ref[row + 1, 0], rs_ref[row + 1, 1] == 1.0
        )
        for i in range(Q):
            l1[row, i] = out[i]
        m2[row, 0] = design
        return 0

    lax.fori_loop(0, ROWS + 2, first, 0)
    for row in range(ROWS):
        designs[pl.ds(row, 8, stride=ROWS), :] = total[row] + m2[row + 1, 0, :, :128]
        mu = pull(l1, row)
        for i in range(Q):
            flat[i, pl.ds(row, 8, stride=ROWS), :] = mu[i][:, :128]
    here = lax.axis_index("gx")
    for k in range(GROUP):
        start = 8 * (here ^ k)
        for i in range(Q + 1):
            outs[k][i] = flat[i, pl.ds(pl.multiple_of(start, 8), 8), :]


def finish_kernel(f_ref, r_ref, s_ref, *refs):
    ins, (lam_ref, sens_ref, blocks) = refs[:GROUP], refs[GROUP:]
    here = lax.axis_index("gx")
    for k in range(GROUP):
        blocks[block_of(here ^ k)] = ins[k][...]
    for half in range(2):
        rows = pl.ds(8 * half, 8)
        for layer in range(LAYERS):
            part = slice(4 * layer, 4 * layer + 4)
            tile = [
                jnp.concatenate([blocks[2 * half, i, part, :], blocks[2 * half + 1, i, part, :]], axis=0)
                for i in range(Q + 1)
            ]
            f = [f_ref[i, layer, rows, :] for i in range(Q)]
            out, design = adjoint_lists(tile[:Q], *moments(f), r_ref[layer, rows, :], s_ref[layer, rows, :] == 1)
            for i in range(Q):
                lam_ref[i, layer, rows, :] = out[i]
            sens_ref[layer, rows, :] = tile[Q] + design


def call(kernel, outs, scratch, *args):
    vmem = pl.BlockSpec(memory_space=pltpu.VMEM)
    return pl.pallas_call(
        kernel,
        out_shape=[jax.ShapeDtypeStruct(shape, jnp.float32) for shape in outs],
        in_specs=[vmem] * len(args),
        out_specs=[vmem] * len(outs),
        scratch_shapes=[pltpu.VMEM(shape, jnp.float32) for shape in scratch],
        compiler_params=pltpu.CompilerParams(vmem_limit_bytes=VMEM_LIMIT),
    )(*args)


def ring_pairs(planes, step):
    gray = [number ^ (number >> 1) for number in range(GROUP)]
    order = []
    for plane in range(planes):
        inside = sorted(range(GROUP), key=lambda number: gray[number])
        order += [(number, plane) for number in (inside if plane % 2 == 0 else inside[::-1])]
    pairs = []
    for at, (number, plane) in enumerate(order):
        other, beyond = order[(at + step) % len(order)]
        pairs.append((number * planes + plane, other * planes + beyond))
    return pairs


def fast_body(checkpoint, resistance, solid, adjoint_final):
    planes = lax.axis_size("gy")

    def trade(pieces):
        moved = [pieces[0]]
        for k in range(1, GROUP):
            moved.append(lax.ppermute(pieces[k], "gx", [(i, i ^ k) for i in range(GROUP)]))
        return moved

    def swap(value):
        return lax.ppermute(value, "gz", [(0, 1), (1, 0)])

    def ring(up, down):
        lo = lax.ppermute(up, ("gx", "gy"), ring_pairs(planes, 1))
        hi = lax.ppermute(down, ("gx", "gy"), ring_pairs(planes, -1))
        return lo, hi

    pieces = call(
        send_kernel, [(FIELDS, 8, 128)] * GROUP, [(GROUP, FIELDS, 8, 128)], checkpoint, resistance, solid, adjoint_final
    )
    pieces = trade(pieces)
    own, up, down = call(
        turn_kernel,
        [(ROWS, FIELDS, 8, 128), (len(FORWARD_UP), 8, 128), (len(FORWARD_DOWN), 8, 128)],
        [(FIELDS, 8 * ROWS, 128)],
        *pieces,
    )
    own_b = swap(own)
    lo, hi = ring(up, down)
    lo_b, hi_b = swap(lo), swap(hi)
    lam, sens, mom1, mom2, rs, up, down = call(
        forward_kernel,
        [
            (ROWS, Q, 8, 256),
            (ROWS, 8, 128),
            (ROWS + 4, 4, 8, 256),
            (ROWS + 4, 4, 8, 256),
            (ROWS + 4, 2, 8, 256),
            (len(BACKWARD_UP), 8, 128),
            (len(BACKWARD_DOWN), 8, 128),
        ],
        [(ROWS + 6, Q, 8, 256), (ROWS + 4, Q, 8, 256), (ROWS + 2, Q, 8, 256), (ROWS + 2, Q, 8, 256)],
        own,
        own_b,
        lo,
        lo_b,
        hi,
        hi_b,
    )
    lo, hi = ring(up, down)
    lo_b, hi_b = swap(lo), swap(hi)
    pieces = call(
        backward_kernel,
        [(Q + 1, 8, 128)] * GROUP,
        [
            (ROWS + 6, Q, 8, 256),
            (ROWS + 4, Q, 8, 256),
            (ROWS + 4, Q, 8, 256),
            (ROWS + 4, 4, 8, 256),
            (Q + 1, 8 * ROWS, 128),
        ],
        lam,
        sens,
        mom1,
        mom2,
        rs,
        lo,
        lo_b,
        hi,
        hi_b,
    )
    pieces = trade(pieces)
    return tuple(
        call(
            finish_kernel,
            [checkpoint.shape, resistance.shape],
            [(GROUP, Q + 1, 8, 128)],
            checkpoint,
            resistance,
            solid,
            *pieces,
        )
    )


def padded_2(shard, sides, width):
    for axis, dim in sides:
        count, length = (lax.axis_size(axis), shard.shape[dim])
        up = [(i, (i + 1) % count) for i in range(count)]
        down = [(j, i) for i, j in up]
        last = lax.slice_in_dim(shard, length - width, length, axis=dim)
        leading = lax.slice_in_dim(shard, 0, width, axis=dim)
        before = lax.ppermute(last, axis, up)
        after = lax.ppermute(leading, axis, down)
        shard = jnp.concatenate([before, shard, after], axis=dim)
    return shard


def collide(populations, resistance, solid):
    lattice = jnp.array(VELOCITIES, jnp.float32)
    weights = jnp.array(WEIGHTS, jnp.float32).reshape(-1, 1, 1, 1)
    density = jnp.sum(populations, axis=0)
    momentum = jnp.tensordot(lattice, populations, axes=([0], [0]), precision=lax.Precision.HIGHEST)
    nothing = jnp.zeros_like(density)
    push = jnp.stack([BODY_FORCE * density, nothing, nothing]) - resistance[None] * momentum
    velocity = (momentum + RELAXATION * push) / density[None]
    projected = jnp.tensordot(lattice, velocity, axes=([1], [0]), precision=lax.Precision.HIGHEST)
    speed_squared = jnp.sum(velocity * velocity, axis=0)
    equilibrium = (
        weights
        * density[None]
        * (1.0 + 3.0 * projected + 4.5 * projected * projected - 1.5 * speed_squared[None])
    )
    relaxed = populations - (populations - equilibrium) / RELAXATION
    reflected = jnp.stack([populations[other] for other in OPPOSITE])
    return jnp.where(solid[None] == 1, reflected, relaxed)


def transport(field, sign):
    padded = padded_2(field, (("gx", 1), ("gy", 2), ("gz", 3)), 1)
    first, second, third = (field.shape[1], field.shape[2], field.shape[3])
    pieces = []
    for number, entry in enumerate(VELOCITIES):
        start_a = 1 - sign * entry[0]
        start_b = 1 - sign * entry[1]
        start_c = 1 - sign * entry[2]
        pieces.append(
            padded[
                number,
                start_a : start_a + first,
                start_b : start_b + second,
                start_c : start_c + third,
            ]
        )
    return jnp.stack(pieces)


def general_body(checkpoint, resistance, solid, adjoint_final):
    states = [checkpoint]
    current = checkpoint
    for step in range(STEPS - 1):
        current = transport(collide(current, resistance, solid), 1)
        states.append(current)
    adjoint = adjoint_final
    sensitivity = jnp.zeros_like(resistance)
    for step in reversed(range(STEPS)):
        pulled = transport(adjoint, -1)

        def local_collide(populations, design):
            return collide(populations, design, solid)

        result, backward = jax.vjp(local_collide, states[step], resistance)
        adjoint, design_part = backward(pulled)
        sensitivity = sensitivity + design_part
    return (adjoint, sensitivity)


def body(checkpoint, resistance, solid, adjoint_final):
    fits = (
        lax.axis_size("gx") == GROUP
        and lax.axis_size("gz") == 2
        and resistance.shape == (LAYERS, GROUP * ROWS, 128)
    )
    chosen = fast_body if fits else general_body
    return chosen(checkpoint, resistance, solid, adjoint_final)


def solution(mesh):
    in_specs = (
        P(None, "gx", "gy", "gz"),
        P("gx", "gy", "gz"),
        P("gx", "gy", "gz"),
        P(None, "gx", "gy", "gz"),
    )
    out_specs = (P(None, "gx", "gy", "gz"), P("gx", "gy", "gz"))
    return jax.shard_map(body, mesh=mesh, in_specs=in_specs, out_specs=out_specs, check_vma=False)
```

```python
import functools

import jax
import jax.numpy as jnp
from jax import lax
from jax.experimental import pallas as pl
from jax.experimental.pallas import tpu as pltpu
from jax.sharding import PartitionSpec as P

STEPS = 4


VELOCITIES = (
    (0, 0, 0),
    (1, 0, 0),
    (-1, 0, 0),
    (0, 1, 0),
    (0, -1, 0),
    (0, 0, 1),
    (0, 0, -1),
    (1, 1, 0),
    (-1, -1, 0),
    (1, -1, 0),
    (-1, 1, 0),
    (1, 0, 1),
    (-1, 0, -1),
    (1, 0, -1),
    (-1, 0, 1),
    (0, 1, 1),
    (0, -1, -1),
    (0, 1, -1),
    (0, -1, 1),
)
WEIGHTS = (1.0 / 3.0,) + (1.0 / 18.0,) * 6 + (1.0 / 36.0,) * 12
OPPOSITE = tuple((VELOCITIES.index((-entry[0], -entry[1], -entry[2])) for entry in VELOCITIES))
RELAXATION = 0.8
BODY_FORCE = 0.01

Q = len(VELOCITIES)
KEEP = 1.0 - 1.0 / RELAXATION
PUSH = RELAXATION * BODY_FORCE
VMEM_LIMIT = 16 * 1024 * 1024

GROUP = 4
ROWS = 4
LAYERS = 2
HALO = 3
RES, SOL, ADJ = Q, Q + 1, Q + 2
FIELDS = Q + 2 + Q

FORWARD_UP = (
    [(3, i, -1) for i in range(Q)]
    + [(2, i, -2) for i in range(Q) if VELOCITIES[i][1] >= 0]
    + [(1, i, -3) for i in range(Q) if VELOCITIES[i][1] > 0]
    + [(3, RES, -1), (3, SOL, -1), (2, RES, -2), (2, SOL, -2)]
    + [(3, ADJ + i, -1) for i in range(Q) if VELOCITIES[i][1] < 0]
)
FORWARD_DOWN = (
    [(0, i, 4) for i in range(Q)]
    + [(1, i, 5) for i in range(Q) if VELOCITIES[i][1] <= 0]
    + [(2, i, 6) for i in range(Q) if VELOCITIES[i][1] < 0]
    + [(0, RES, 4), (0, SOL, 4), (1, RES, 5), (1, SOL, 5)]
    + [(0, ADJ + i, 4) for i in range(Q) if VELOCITIES[i][1] > 0]
)
BACKWARD_UP = (
    [(3, i, -1) for i in range(Q)]
    + [(2, i, -2) for i in range(Q) if VELOCITIES[i][1] <= 0]
    + [(1, i, -3) for i in range(Q) if VELOCITIES[i][1] < 0]
    + [(2, Q + j, -2) for j in range(4)]
)
BACKWARD_DOWN = (
    [(0, i, 4) for i in range(Q)]
    + [(1, i, 5) for i in range(Q) if VELOCITIES[i][1] >= 0]
    + [(2, i, 6) for i in range(Q) if VELOCITIES[i][1] > 0]
    + [(1, Q + j, 5) for j in range(4)]
)


def moments(f):
    plus = [f[i] + f[i + 1] for i in range(1, Q, 2)]
    less = [f[i] - f[i + 1] for i in range(1, Q, 2)]
    density = f[0] + ((plus[0] + plus[1]) + (plus[2] + plus[3])) + ((plus[4] + plus[5]) + (plus[6] + (plus[7] + plus[8])))
    first = less[0] + ((less[3] + less[4]) + (less[5] + less[6]))
    second = less[1] + ((less[3] - less[4]) + (less[7] + less[8]))
    third = less[2] + ((less[5] - less[6]) + (less[7] - less[8]))
    inverse = 1.0 / density
    return density, first * inverse, second * inverse, third * inverse


def along(i, x, y, z):
    total = None
    for sign, part in zip(VELOCITIES[i], (x, y, z)):
        if sign == 0:
            continue
        if total is None:
            total = part if sign > 0 else -part
        else:
            total = total + part if sign > 0 else total - part
    return total


def collide_lists(f, density, vx, vy, vz, resistance, solid):
    damp = 1.0 - RELAXATION * resistance
    ux, uy, uz = damp * vx + PUSH, damp * vy, damp * vz
    base = 1.0 - 1.5 * (ux * ux + uy * uy + uz * uz)
    scaled = {w: density * (w / RELAXATION) for w in sorted(set(WEIGHTS))}
    out = [jnp.where(solid, f[0], KEEP * f[0] + scaled[WEIGHTS[0]] * base)]
    for i in range(1, Q, 2):
        projected = along(i, ux, uy, uz)
        weight = scaled[WEIGHTS[i]]
        even = weight * (base + 4.5 * (projected * projected))
        odd = weight * (3.0 * projected)
        out.append(jnp.where(solid, f[i + 1], KEEP * f[i] + (even + odd)))
        out.append(jnp.where(solid, f[i], KEEP * f[i + 1] + (even - odd)))
    return out


def adjoint_lists(mu, density, vx, vy, vz, resistance, solid):
    damp = 1.0 - RELAXATION * resistance
    ux, uy, uz = damp * vx + PUSH, damp * vy, damp * vz
    plus = [mu[i] + mu[i + 1] for i in range(1, Q, 2)]
    less = [mu[i] - mu[i + 1] for i in range(1, Q, 2)]
    rest, axis, diagonal = (w / RELAXATION for w in (WEIGHTS[0], WEIGHTS[1], WEIGHTS[7]))
    xy, xz, yz = plus[3] + plus[4], plus[5] + plus[6], plus[7] + plus[8]
    zeroth = rest * mu[0] + axis * ((plus[0] + plus[1]) + plus[2]) + diagonal * ((xy + xz) + yz)
    nx = axis * less[0] + diagonal * ((less[3] + less[4]) + (less[5] + less[6]))
    ny = axis * less[1] + diagonal * ((less[3] - less[4]) + (less[7] + less[8]))
    nz = axis * less[2] + diagonal * ((less[5] - less[6]) + (less[7] - less[8]))
    nxx = axis * plus[0] + diagonal * (xy + xz)
    nyy = axis * plus[1] + diagonal * (xy + yz)
    nzz = axis * plus[2] + diagonal * (xz + yz)
    nxy = diagonal * (plus[3] - plus[4])
    nxz = diagonal * (plus[5] - plus[6])
    nyz = diagonal * (plus[7] - plus[8])
    tx = nxx * ux + nxy * uy + nxz * uz
    ty = nxy * ux + nyy * uy + nyz * uz
    tz = nxz * ux + nyz * uy + nzz * uz
    hx = 3.0 * (nx - ux * zeroth) + 9.0 * tx
    hy = 3.0 * (ny - uy * zeroth) + 9.0 * ty
    hz = 3.0 * (nz - uz * zeroth) + 9.0 * tz
    pulled = vx * hx + vy * hy + vz * hz
    square = ux * ux + uy * uy + uz * uz
    scalar = (
        zeroth * (1.0 - 1.5 * square)
        + 3.0 * (nx * ux + ny * uy + nz * uz)
        + 4.5 * (tx * ux + ty * uy + tz * uz)
        - damp * pulled
    )
    qx, qy, qz = damp * hx, damp * hy, damp * hz
    out = [jnp.where(solid, mu[0], KEEP * mu[0] + scalar)]
    for i in range(1, Q, 2):
        slope = along(i, qx, qy, qz)
        out.append(jnp.where(solid, mu[i + 1], KEEP * mu[i] + (scalar + slope)))
        out.append(jnp.where(solid, mu[i], KEEP * mu[i + 1] + (scalar - slope)))
    design = jnp.where(solid, 0.0, (-RELAXATION) * density * pulled)
    return out, design


def shifted(value, i, sign):
    first, _, third = VELOCITIES[i]
    if first:
        value = pltpu.roll(value, (sign * first) % value.shape[0], axis=0)
    if third:
        value = pltpu.roll(value, (sign * third) % value.shape[1], axis=1)
    return value


def block_of(number):
    return (lax.axis_index("gy") + GROUP - (number ^ (number >> 1))) % GROUP


def send_kernel(*refs):
    given, outs, blocks, held, sems = refs[:4], refs[4 : 4 + GROUP], refs[4 + GROUP], refs[5 + GROUP : 9 + GROUP], refs[-1]
    copies = [pltpu.make_async_copy(source, target, sems.at[at]) for at, (source, target) in enumerate(zip(given, held))]
    for copy in copies:
        copy.start()
    for copy in copies:
        copy.wait()
    f_ref, r_ref, s_ref, a_ref = held
    for half in range(2):
        rows = pl.ds(8 * half, 8)
        tiles = []
        for layer in range(LAYERS):
            f = [f_ref[i, layer, rows, :] for i in range(Q)]
            resistance, kind = r_ref[layer, rows, :], s_ref[layer, rows, :]
            out = collide_lists(f, *moments(f), resistance, kind == 1)
            out += [resistance, kind.astype(jnp.float32)]
            out += [a_ref[i, layer, rows, :] for i in range(Q)]
            tiles.append(out)
        for field in range(FIELDS):
            first, second = tiles[0][field], tiles[1][field]
            blocks[2 * half, field] = jnp.concatenate([first[:4], second[:4]], axis=0)
            blocks[2 * half + 1, field] = jnp.concatenate([first[4:], second[4:]], axis=0)
    here = lax.axis_index("gx")
    for k in range(GROUP):
        outs[k][...] = blocks[block_of(here ^ k)]


def turn_kernel(*refs):
    ins, (own, up, down, flat) = refs[:GROUP], refs[GROUP:]
    here = lax.axis_index("gx")
    for k in range(GROUP):
        start = 8 * (here ^ k)
        for field in range(FIELDS):
            flat[field, pl.ds(pl.multiple_of(start, 8), 8), :] = ins[k][field]
    for field in range(FIELDS):
        for row in range(ROWS):
            own[row, field] = flat[field, pl.ds(row, 8, stride=ROWS), :]
    for number, (row, field, _) in enumerate(FORWARD_UP):
        up[number] = own[row, field]
    for number, (row, field, _) in enumerate(FORWARD_DOWN):
        down[number] = own[row, field]


def forward_kernel(own_a, own_b, lo_a, lo_b, hi_a, hi_b, lam_ref, sens_ref, mom1, mom2, rs_ref, up, down, p0, p1, p2, a4):
    for side, own, lo, hi in ((0, own_a, lo_a, hi_a), (1, own_b, lo_b, hi_b)):
        lanes = slice(128 * side, 128 * side + 128)
        for row in range(ROWS):
            for i in range(Q):
                p0[row + 3, i, :, lanes] = own[row, i]
                a4[row + 1, i, :, lanes] = own[row, ADJ + i]
            for j in range(2):
                rs_ref[row + 2, j, :, lanes] = own[row, RES + j]
        for table, part in ((FORWARD_UP, lo), (FORWARD_DOWN, hi)):
            for number, (_, field, row) in enumerate(table):
                if field < Q:
                    p0[row + 3, field, :, lanes] = part[number]
                elif field < ADJ:
                    rs_ref[row + 2, field - RES, :, lanes] = part[number]
                else:
                    a4[row + 1, field - ADJ, :, lanes] = part[number]

    def pull(source, row):
        return [shifted(source[row + 1 - VELOCITIES[i][1], i], i, 1) for i in range(Q)]

    def first(row, _):
        f = pull(p0, row)
        moment = moments(f)
        for j in range(4):
            mom1[row, j] = moment[j]
        out = collide_lists(f, *moment, rs_ref[row, 0], rs_ref[row, 1] == 1.0)
        for i in range(Q):
            p1[row, i] = out[i]
        return 0

    lax.fori_loop(0, ROWS + 4, first, 0)

    def second(row, _):
        f = pull(p1, row)
        moment = moments(f)
        for j in range(4):
            mom2[row + 1, j] = moment[j]
        out = collide_lists(f, *moment, rs_ref[row + 1, 0], rs_ref[row + 1, 1] == 1.0)
        for i in range(Q):
            p2[row, i] = out[i]
        return 0

    lax.fori_loop(0, ROWS + 2, second, 0)

    def third(row, _):
        moment = moments(pull(p2, row))
        mu = [shifted(a4[row + 1 + VELOCITIES[i][1], i], i, -1) for i in range(Q)]
        out, design = adjoint_lists(mu, *moment, rs_ref[row + 2, 0], rs_ref[row + 2, 1] == 1.0)
        for i in range(Q):
            lam_ref[row, i] = out[i]
        sens_ref[row] = design[:, :128]
        return 0

    lax.fori_loop(0, ROWS, third, 0)
    for table, part in ((BACKWARD_UP, up), (BACKWARD_DOWN, down)):
        for number, (row, field, _) in enumerate(table):
            source = lam_ref[row, field, :, :128] if field < Q else mom2[row + 2, field - Q, :, :128]
            part[number] = source
    for row in (0, ROWS + 3):
        for j in range(4):
            mom2[row, j] = jnp.zeros((8, 256), jnp.float32)


def backward_kernel(lam_ref, sens_ref, mom1, mom2, rs_ref, lo_a, lo_b, hi_a, hi_b, *refs):
    outs, (l3, l2, l1, m2, flat) = refs[:GROUP], refs[GROUP:]
    for row in range(ROWS):
        for i in range(Q):
            l3[row + 3, i] = lam_ref[row, i]
    for row in range(ROWS + 4):
        for j in range(4):
            m2[row, j] = mom2[row, j]
    for side, lo, hi in ((0, lo_a, hi_a), (1, lo_b, hi_b)):
        lanes = slice(128 * side, 128 * side + 128)
        for table, part in ((BACKWARD_UP, lo), (BACKWARD_DOWN, hi)):
            for number, (_, field, row) in enumerate(table):
                if field < Q:
                    l3[row + 3, field, :, lanes] = part[number]
                else:
                    m2[row + 2, field - Q, :, lanes] = part[number]

    def pull(source, row):
        return [shifted(source[row + 1 + VELOCITIES[i][1], i], i, -1) for i in range(Q)]

    designs = flat.at[Q]

    def second(row, _):
        mu = pull(l3, row)
        out, design = adjoint_lists(mu, *[m2[row, j] for j in range(4)], rs_ref[row, 0], rs_ref[row, 1] == 1.0)
        for i in range(Q):
            l2[row, i] = out[i]
        l1[row, 0] = design
        return 0

    lax.fori_loop(0, ROWS + 4, second, 0)
    total = [sens_ref[row] + l1[row + 2, 0, :, :128] for row in range(ROWS)]

    def first(row, _):
        mu = pull(l2, row)
        out, design = adjoint_lists(
            mu, *[mom1[row + 1, j] for j in range(4)], rs_ref[row + 1, 0], rs_ref[row + 1, 1] == 1.0
        )
        for i in range(Q):
            l1[row, i] = out[i]
        m2[row, 0] = design
        return 0

    lax.fori_loop(0, ROWS + 2, first, 0)
    for row in range(ROWS):
        designs[pl.ds(row, 8, stride=ROWS), :] = total[row] + m2[row + 1, 0, :, :128]
        mu = pull(l1, row)
        for i in range(Q):
            flat[i, pl.ds(row, 8, stride=ROWS), :] = mu[i][:, :128]
    here = lax.axis_index("gx")
    for k in range(GROUP):
        start = 8 * (here ^ k)
        for i in range(Q + 1):
            outs[k][i] = flat[i, pl.ds(pl.multiple_of(start, 8), 8), :]


def finish_kernel(f_ref, r_ref, s_ref, *refs):
    ins, (lam_ref, sens_ref, blocks) = refs[:GROUP], refs[GROUP:]
    here = lax.axis_index("gx")
    for k in range(GROUP):
        blocks[block_of(here ^ k)] = ins[k][...]
    for half in range(2):
        rows = pl.ds(8 * half, 8)
        for layer in range(LAYERS):
            part = slice(4 * layer, 4 * layer + 4)
            tile = [
                jnp.concatenate([blocks[2 * half, i, part, :], blocks[2 * half + 1, i, part, :]], axis=0)
                for i in range(Q + 1)
            ]
            f = [f_ref[i, layer, rows, :] for i in range(Q)]
            out, design = adjoint_lists(tile[:Q], *moments(f), r_ref[layer, rows, :], s_ref[layer, rows, :] == 1)
            for i in range(Q):
                lam_ref[i, layer, rows, :] = out[i]
            sens_ref[layer, rows, :] = tile[Q] + design


def call(kernel, outs, scratch, *args, space=pltpu.VMEM):
    vmem = pl.BlockSpec(memory_space=pltpu.VMEM)
    return pl.pallas_call(
        kernel,
        out_shape=[jax.ShapeDtypeStruct(shape, jnp.float32) for shape in outs],
        in_specs=[pl.BlockSpec(memory_space=space)] * len(args),
        out_specs=[vmem] * len(outs),
        scratch_shapes=[pltpu.VMEM(shape, jnp.float32) if isinstance(shape, tuple) else shape for shape in scratch],
        compiler_params=pltpu.CompilerParams(vmem_limit_bytes=VMEM_LIMIT),
    )(*args)


def ring_pairs(planes, step):
    order = []
    for plane in range(planes):
        for block in range(GROUP):
            gray = (plane - block) % GROUP
            order.append((gray ^ (gray >> 1), plane))
    pairs = []
    for at, (number, plane) in enumerate(order):
        other, beyond = order[(at + step) % len(order)]
        pairs.append((number * planes + plane, other * planes + beyond))
    return pairs


def fast_body(checkpoint, resistance, solid, adjoint_final):
    planes = lax.axis_size("gy")

    def trade(pieces):
        moved = [pieces[0]]
        for k in range(1, GROUP):
            moved.append(lax.ppermute(pieces[k], "gx", [(i, i ^ k) for i in range(GROUP)]))
        return moved

    def swap(value):
        return lax.ppermute(value, "gz", [(0, 1), (1, 0)])

    def ring(up, down):
        lo = lax.ppermute(up, ("gx", "gy"), ring_pairs(planes, 1))
        hi = lax.ppermute(down, ("gx", "gy"), ring_pairs(planes, -1))
        return lo, hi

    given = (checkpoint, resistance, solid, adjoint_final)
    pieces = call(
        send_kernel,
        [(FIELDS, 8, 128)] * GROUP,
        [(GROUP, FIELDS, 8, 128)]
        + [pltpu.VMEM(array.shape, array.dtype) for array in given]
        + [pltpu.SemaphoreType.DMA((len(given),))],
        *[pltpu.with_memory_space_constraint(array, pltpu.HBM) for array in given],
        space=pltpu.HBM,
    )
    pieces = trade(pieces)
    own, up, down = call(
        turn_kernel,
        [(ROWS, FIELDS, 8, 128), (len(FORWARD_UP), 8, 128), (len(FORWARD_DOWN), 8, 128)],
        [(FIELDS, 8 * ROWS, 128)],
        *pieces,
    )
    own_b = swap(own)
    lo, hi = ring(up, down)
    lo_b, hi_b = swap(lo), swap(hi)
    lam, sens, mom1, mom2, rs, up, down = call(
        forward_kernel,
        [
            (ROWS, Q, 8, 256),
            (ROWS, 8, 128),
            (ROWS + 4, 4, 8, 256),
            (ROWS + 4, 4, 8, 256),
            (ROWS + 4, 2, 8, 256),
            (len(BACKWARD_UP), 8, 128),
            (len(BACKWARD_DOWN), 8, 128),
        ],
        [(ROWS + 6, Q, 8, 256), (ROWS + 4, Q, 8, 256), (ROWS + 2, Q, 8, 256), (ROWS + 2, Q, 8, 256)],
        own,
        own_b,
        lo,
        lo_b,
        hi,
        hi_b,
    )
    lo, hi = ring(up, down)
    lo_b, hi_b = swap(lo), swap(hi)
    pieces = call(
        backward_kernel,
        [(Q + 1, 8, 128)] * GROUP,
        [
            (ROWS + 6, Q, 8, 256),
            (ROWS + 4, Q, 8, 256),
            (ROWS + 4, Q, 8, 256),
            (ROWS + 4, 4, 8, 256),
            (Q + 1, 8 * ROWS, 128),
        ],
        lam,
        sens,
        mom1,
        mom2,
        rs,
        lo,
        lo_b,
        hi,
        hi_b,
    )
    pieces = trade(pieces)
    return tuple(
        call(
            finish_kernel,
            [checkpoint.shape, resistance.shape],
            [(GROUP, Q + 1, 8, 128)],
            checkpoint,
            resistance,
            solid,
            *pieces,
        )
    )


def padded_2(shard, sides, width):
    for axis, dim in sides:
        count, length = (lax.axis_size(axis), shard.shape[dim])
        up = [(i, (i + 1) % count) for i in range(count)]
        down = [(j, i) for i, j in up]
        last = lax.slice_in_dim(shard, length - width, length, axis=dim)
        leading = lax.slice_in_dim(shard, 0, width, axis=dim)
        before = lax.ppermute(last, axis, up)
        after = lax.ppermute(leading, axis, down)
        shard = jnp.concatenate([before, shard, after], axis=dim)
    return shard


def collide(populations, resistance, solid):
    lattice = jnp.array(VELOCITIES, jnp.float32)
    weights = jnp.array(WEIGHTS, jnp.float32).reshape(-1, 1, 1, 1)
    density = jnp.sum(populations, axis=0)
    momentum = jnp.tensordot(lattice, populations, axes=([0], [0]), precision=lax.Precision.HIGHEST)
    nothing = jnp.zeros_like(density)
    push = jnp.stack([BODY_FORCE * density, nothing, nothing]) - resistance[None] * momentum
    velocity = (momentum + RELAXATION * push) / density[None]
    projected = jnp.tensordot(lattice, velocity, axes=([1], [0]), precision=lax.Precision.HIGHEST)
    speed_squared = jnp.sum(velocity * velocity, axis=0)
    equilibrium = (
        weights
        * density[None]
        * (1.0 + 3.0 * projected + 4.5 * projected * projected - 1.5 * speed_squared[None])
    )
    relaxed = populations - (populations - equilibrium) / RELAXATION
    reflected = jnp.stack([populations[other] for other in OPPOSITE])
    return jnp.where(solid[None] == 1, reflected, relaxed)


def transport(field, sign):
    padded = padded_2(field, (("gx", 1), ("gy", 2), ("gz", 3)), 1)
    first, second, third = (field.shape[1], field.shape[2], field.shape[3])
    pieces = []
    for number, entry in enumerate(VELOCITIES):
        start_a = 1 - sign * entry[0]
        start_b = 1 - sign * entry[1]
        start_c = 1 - sign * entry[2]
        pieces.append(
            padded[
                number,
                start_a : start_a + first,
                start_b : start_b + second,
                start_c : start_c + third,
            ]
        )
    return jnp.stack(pieces)


def general_body(checkpoint, resistance, solid, adjoint_final):
    states = [checkpoint]
    current = checkpoint
    for step in range(STEPS - 1):
        current = transport(collide(current, resistance, solid), 1)
        states.append(current)
    adjoint = adjoint_final
    sensitivity = jnp.zeros_like(resistance)
    for step in reversed(range(STEPS)):
        pulled = transport(adjoint, -1)

        def local_collide(populations, design):
            return collide(populations, design, solid)

        result, backward = jax.vjp(local_collide, states[step], resistance)
        adjoint, design_part = backward(pulled)
        sensitivity = sensitivity + design_part
    return (adjoint, sensitivity)


def body(checkpoint, resistance, solid, adjoint_final):
    fits = (
        lax.axis_size("gx") == GROUP
        and lax.axis_size("gz") == 2
        and resistance.shape == (LAYERS, GROUP * ROWS, 128)
    )
    chosen = fast_body if fits else general_body
    return chosen(checkpoint, resistance, solid, adjoint_final)


def solution(mesh):
    in_specs = (
        P(None, "gx", "gy", "gz"),
        P("gx", "gy", "gz"),
        P("gx", "gy", "gz"),
        P(None, "gx", "gy", "gz"),
    )
    out_specs = (P(None, "gx", "gy", "gz"), P("gx", "gy", "gz"))
    return jax.shard_map(body, mesh=mesh, in_specs=in_specs, out_specs=out_specs, check_vma=False)
```

```python
import functools

import jax
import jax.numpy as jnp
from jax import lax
from jax.experimental import pallas as pl
from jax.experimental.pallas import tpu as pltpu
from jax.sharding import PartitionSpec as P

STEPS = 4


VELOCITIES = (
    (0, 0, 0),
    (1, 0, 0),
    (-1, 0, 0),
    (0, 1, 0),
    (0, -1, 0),
    (0, 0, 1),
    (0, 0, -1),
    (1, 1, 0),
    (-1, -1, 0),
    (1, -1, 0),
    (-1, 1, 0),
    (1, 0, 1),
    (-1, 0, -1),
    (1, 0, -1),
    (-1, 0, 1),
    (0, 1, 1),
    (0, -1, -1),
    (0, 1, -1),
    (0, -1, 1),
)
WEIGHTS = (1.0 / 3.0,) + (1.0 / 18.0,) * 6 + (1.0 / 36.0,) * 12
OPPOSITE = tuple((VELOCITIES.index((-entry[0], -entry[1], -entry[2])) for entry in VELOCITIES))
RELAXATION = 0.8
BODY_FORCE = 0.01

Q = len(VELOCITIES)
KEEP = 1.0 - 1.0 / RELAXATION
PUSH = RELAXATION * BODY_FORCE
VMEM_LIMIT = 16 * 1024 * 1024

GROUP = 4
ROWS = 4
LAYERS = 2
HALO = 3
WIDTH = 2 * HALO
SLOTS = 128 // WIDTH
RES, SOL, ADJ = Q, Q + 1, Q + 2
FIELDS = Q + 2 + Q

FORWARD_UP = (
    [(3, i, -1) for i in range(Q)]
    + [(2, i, -2) for i in range(Q) if VELOCITIES[i][1] >= 0]
    + [(1, i, -3) for i in range(Q) if VELOCITIES[i][1] > 0]
    + [(3, RES, -1), (3, SOL, -1), (2, RES, -2), (2, SOL, -2)]
    + [(3, ADJ + i, -1) for i in range(Q) if VELOCITIES[i][1] < 0]
)
FORWARD_DOWN = (
    [(0, i, 4) for i in range(Q)]
    + [(1, i, 5) for i in range(Q) if VELOCITIES[i][1] <= 0]
    + [(2, i, 6) for i in range(Q) if VELOCITIES[i][1] < 0]
    + [(0, RES, 4), (0, SOL, 4), (1, RES, 5), (1, SOL, 5)]
    + [(0, ADJ + i, 4) for i in range(Q) if VELOCITIES[i][1] > 0]
)
BACKWARD_UP = (
    [(3, i, -1) for i in range(Q)]
    + [(2, i, -2) for i in range(Q) if VELOCITIES[i][1] <= 0]
    + [(1, i, -3) for i in range(Q) if VELOCITIES[i][1] < 0]
    + [(2, Q + j, -2) for j in range(4)]
)
BACKWARD_DOWN = (
    [(0, i, 4) for i in range(Q)]
    + [(1, i, 5) for i in range(Q) if VELOCITIES[i][1] >= 0]
    + [(2, i, 6) for i in range(Q) if VELOCITIES[i][1] > 0]
    + [(1, Q + j, 5) for j in range(4)]
)


def moments(f):
    plus = [f[i] + f[i + 1] for i in range(1, Q, 2)]
    less = [f[i] - f[i + 1] for i in range(1, Q, 2)]
    density = f[0] + ((plus[0] + plus[1]) + (plus[2] + plus[3])) + ((plus[4] + plus[5]) + (plus[6] + (plus[7] + plus[8])))
    first = less[0] + ((less[3] + less[4]) + (less[5] + less[6]))
    second = less[1] + ((less[3] - less[4]) + (less[7] + less[8]))
    third = less[2] + ((less[5] - less[6]) + (less[7] - less[8]))
    inverse = 1.0 / density
    return density, first * inverse, second * inverse, third * inverse


def strip_count(table):
    return -(-len(table) // SLOTS)


def pack_strips(tiles):
    lane = lax.broadcasted_iota(jnp.int32, (8, 128), 1)
    packed = []
    for number, tile in enumerate(tiles):
        slot = number % SLOTS
        moved = pltpu.roll(tile, (WIDTH * slot + HALO) % 128, axis=1)
        if slot == 0:
            packed.append(moved)
        else:
            packed[-1] = jnp.where(lane >= WIDTH * slot, moved, packed[-1])
    return packed


def unpack_strip(packed, number):
    return pltpu.roll(packed, (-WIDTH * (number % SLOTS) - HALO) % 128, axis=1)


def along(i, x, y, z):
    total = None
    for sign, part in zip(VELOCITIES[i], (x, y, z)):
        if sign == 0:
            continue
        if total is None:
            total = part if sign > 0 else -part
        else:
            total = total + part if sign > 0 else total - part
    return total


def collide_lists(f, density, vx, vy, vz, resistance, solid):
    damp = 1.0 - RELAXATION * resistance
    ux, uy, uz = damp * vx + PUSH, damp * vy, damp * vz
    base = 1.0 - 1.5 * (ux * ux + uy * uy + uz * uz)
    scaled = {w: density * (w / RELAXATION) for w in sorted(set(WEIGHTS))}
    out = [jnp.where(solid, f[0], KEEP * f[0] + scaled[WEIGHTS[0]] * base)]
    for i in range(1, Q, 2):
        projected = along(i, ux, uy, uz)
        weight = scaled[WEIGHTS[i]]
        even = weight * (base + 4.5 * (projected * projected))
        odd = weight * (3.0 * projected)
        out.append(jnp.where(solid, f[i + 1], KEEP * f[i] + (even + odd)))
        out.append(jnp.where(solid, f[i], KEEP * f[i + 1] + (even - odd)))
    return out


def adjoint_lists(mu, density, vx, vy, vz, resistance, solid):
    damp = 1.0 - RELAXATION * resistance
    ux, uy, uz = damp * vx + PUSH, damp * vy, damp * vz
    plus = [mu[i] + mu[i + 1] for i in range(1, Q, 2)]
    less = [mu[i] - mu[i + 1] for i in range(1, Q, 2)]
    rest, axis, diagonal = (w / RELAXATION for w in (WEIGHTS[0], WEIGHTS[1], WEIGHTS[7]))
    xy, xz, yz = plus[3] + plus[4], plus[5] + plus[6], plus[7] + plus[8]
    zeroth = rest * mu[0] + axis * ((plus[0] + plus[1]) + plus[2]) + diagonal * ((xy + xz) + yz)
    nx = axis * less[0] + diagonal * ((less[3] + less[4]) + (less[5] + less[6]))
    ny = axis * less[1] + diagonal * ((less[3] - less[4]) + (less[7] + less[8]))
    nz = axis * less[2] + diagonal * ((less[5] - less[6]) + (less[7] - less[8]))
    nxx = axis * plus[0] + diagonal * (xy + xz)
    nyy = axis * plus[1] + diagonal * (xy + yz)
    nzz = axis * plus[2] + diagonal * (xz + yz)
    nxy = diagonal * (plus[3] - plus[4])
    nxz = diagonal * (plus[5] - plus[6])
    nyz = diagonal * (plus[7] - plus[8])
    tx = nxx * ux + nxy * uy + nxz * uz
    ty = nxy * ux + nyy * uy + nyz * uz
    tz = nxz * ux + nyz * uy + nzz * uz
    hx = 3.0 * (nx - ux * zeroth) + 9.0 * tx
    hy = 3.0 * (ny - uy * zeroth) + 9.0 * ty
    hz = 3.0 * (nz - uz * zeroth) + 9.0 * tz
    pulled = vx * hx + vy * hy + vz * hz
    square = ux * ux + uy * uy + uz * uz
    scalar = (
        zeroth * (1.0 - 1.5 * square)
        + 3.0 * (nx * ux + ny * uy + nz * uz)
        + 4.5 * (tx * ux + ty * uy + tz * uz)
        - damp * pulled
    )
    qx, qy, qz = damp * hx, damp * hy, damp * hz
    out = [jnp.where(solid, mu[0], KEEP * mu[0] + scalar)]
    for i in range(1, Q, 2):
        slope = along(i, qx, qy, qz)
        out.append(jnp.where(solid, mu[i + 1], KEEP * mu[i] + (scalar + slope)))
        out.append(jnp.where(solid, mu[i], KEEP * mu[i + 1] + (scalar - slope)))
    design = jnp.where(solid, 0.0, (-RELAXATION) * density * pulled)
    return out, design


def shifted(value, i, sign):
    first, _, third = VELOCITIES[i]
    if first:
        value = pltpu.roll(value, (sign * first) % value.shape[0], axis=0)
    if third:
        value = pltpu.roll(value, (sign * third) % value.shape[1], axis=1)
    return value


def block_of(number):
    return (lax.axis_index("gy") + GROUP - (number ^ (number >> 1))) % GROUP


def send_kernel(*refs):
    given, outs, blocks, held, sems = refs[:4], refs[4 : 4 + GROUP], refs[4 + GROUP], refs[5 + GROUP : 9 + GROUP], refs[-1]
    copies = [pltpu.make_async_copy(source, target, sems.at[at]) for at, (source, target) in enumerate(zip(given, held))]
    for copy in copies:
        copy.start()
    for copy in copies:
        copy.wait()
    f_ref, r_ref, s_ref, a_ref = held
    for half in range(2):
        rows = pl.ds(8 * half, 8)
        tiles = []
        for layer in range(LAYERS):
            f = [f_ref[i, layer, rows, :] for i in range(Q)]
            resistance, kind = r_ref[layer, rows, :], s_ref[layer, rows, :]
            out = collide_lists(f, *moments(f), resistance, kind == 1)
            out += [resistance, kind.astype(jnp.float32)]
            out += [a_ref[i, layer, rows, :] for i in range(Q)]
            tiles.append(out)
        for field in range(FIELDS):
            first, second = tiles[0][field], tiles[1][field]
            blocks[2 * half, field] = jnp.concatenate([first[:4], second[:4]], axis=0)
            blocks[2 * half + 1, field] = jnp.concatenate([first[4:], second[4:]], axis=0)
    here = lax.axis_index("gx")
    for k in range(GROUP):
        outs[k][...] = blocks[block_of(here ^ k)]


def turn_kernel(*refs):
    ins, (own, up, down, flat) = refs[:GROUP], refs[GROUP:]
    here = lax.axis_index("gx")
    for k in range(GROUP):
        start = 8 * (here ^ k)
        for field in range(FIELDS):
            flat[field, pl.ds(pl.multiple_of(start, 8), 8), :] = ins[k][field]
    for field in range(FIELDS):
        for row in range(ROWS):
            own[row, field] = flat[field, pl.ds(row, 8, stride=ROWS), :]
    for number, (row, field, _) in enumerate(FORWARD_UP):
        up[number] = own[row, field]
    for number, (row, field, _) in enumerate(FORWARD_DOWN):
        down[number] = own[row, field]


def forward_kernel(own_a, own_b, lo_a, lo_b, hi_a, hi_b, lam_ref, sens_ref, mom1, mom2, rs_ref, up, down, p0, p1, p2, a4):
    for side, own, lo, hi in ((0, own_a, lo_a, hi_a), (1, own_b, lo_b, hi_b)):
        lanes = slice(128 * side, 128 * side + 128)
        for row in range(ROWS):
            for i in range(Q):
                p0[row + 3, i, :, lanes] = own[row, i]
                a4[row + 1, i, :, lanes] = own[row, ADJ + i]
            for j in range(2):
                rs_ref[row + 2, j, :, lanes] = own[row, RES + j]
        for table, part in ((FORWARD_UP, lo), (FORWARD_DOWN, hi)):
            for number, (_, field, row) in enumerate(table):
                if field < Q:
                    p0[row + 3, field, :, lanes] = part[number]
                elif field < ADJ:
                    rs_ref[row + 2, field - RES, :, lanes] = part[number]
                else:
                    a4[row + 1, field - ADJ, :, lanes] = part[number]

    def pull(source, row):
        return [shifted(source[row + 1 - VELOCITIES[i][1], i], i, 1) for i in range(Q)]

    def first(row, _):
        f = pull(p0, row)
        moment = moments(f)
        for j in range(4):
            mom1[row, j] = moment[j]
        out = collide_lists(f, *moment, rs_ref[row, 0], rs_ref[row, 1] == 1.0)
        for i in range(Q):
            p1[row, i] = out[i]
        return 0

    lax.fori_loop(0, ROWS + 4, first, 0, unroll=True)

    def second(row, _):
        f = pull(p1, row)
        moment = moments(f)
        for j in range(4):
            mom2[row + 1, j] = moment[j]
        out = collide_lists(f, *moment, rs_ref[row + 1, 0], rs_ref[row + 1, 1] == 1.0)
        for i in range(Q):
            p2[row, i] = out[i]
        return 0

    lax.fori_loop(0, ROWS + 2, second, 0, unroll=True)

    def third(row, _):
        moment = moments(pull(p2, row))
        mu = [shifted(a4[row + 1 + VELOCITIES[i][1], i], i, -1) for i in range(Q)]
        out, design = adjoint_lists(mu, *moment, rs_ref[row + 2, 0], rs_ref[row + 2, 1] == 1.0)
        for i in range(Q):
            lam_ref[row, i] = out[i]
        sens_ref[row] = design[:, :128]
        return 0

    lax.fori_loop(0, ROWS, third, 0, unroll=True)
    for table, part in ((BACKWARD_UP, up), (BACKWARD_DOWN, down)):
        others = []
        for number, (row, field, _) in enumerate(table):
            source = lam_ref[row, field] if field < Q else mom2[row + 2, field - Q]
            part[number] = source[:, :128]
            others.append(source[:, 128:])
        for number, tile in enumerate(pack_strips(others)):
            part[len(table) + number] = tile
    for row in (0, ROWS + 3):
        for j in range(4):
            mom2[row, j] = jnp.zeros((8, 256), jnp.float32)


def backward_kernel(lam_ref, sens_ref, mom1, mom2, rs_ref, lo, hi, *refs):
    outs, (l3, l2, l1, m2, flat) = refs[:GROUP], refs[GROUP:]
    for row in range(ROWS):
        for i in range(Q):
            l3[row + 3, i] = lam_ref[row, i]
    for row in range(ROWS + 4):
        for j in range(4):
            m2[row, j] = mom2[row, j]
    for table, part in ((BACKWARD_UP, lo), (BACKWARD_DOWN, hi)):
        packed = [part[len(table) + number] for number in range(strip_count(table))]
        for number, (_, field, row) in enumerate(table):
            target = l3.at[row + 3, field] if field < Q else m2.at[row + 2, field - Q]
            target[:, :128] = part[number]
            target[:, 128:] = unpack_strip(packed[number // SLOTS], number)

    def pull(source, row):
        return [shifted(source[row + 1 + VELOCITIES[i][1], i], i, -1) for i in range(Q)]

    designs = flat.at[Q]

    def second(row, _):
        mu = pull(l3, row)
        out, design = adjoint_lists(mu, *[m2[row, j] for j in range(4)], rs_ref[row, 0], rs_ref[row, 1] == 1.0)
        for i in range(Q):
            l2[row, i] = out[i]
        l1[row, 0] = design
        return 0

    lax.fori_loop(0, ROWS + 4, second, 0, unroll=True)
    total = [sens_ref[row] + l1[row + 2, 0, :, :128] for row in range(ROWS)]

    def first(row, _):
        mu = pull(l2, row)
        out, design = adjoint_lists(
            mu, *[mom1[row + 1, j] for j in range(4)], rs_ref[row + 1, 0], rs_ref[row + 1, 1] == 1.0
        )
        for i in range(Q):
            l1[row, i] = out[i]
        m2[row, 0] = design
        return 0

    lax.fori_loop(0, ROWS + 2, first, 0, unroll=True)
    for row in range(ROWS):
        designs[pl.ds(row, 8, stride=ROWS), :] = total[row] + m2[row + 1, 0, :, :128]
        mu = pull(l1, row)
        for i in range(Q):
            flat[i, pl.ds(row, 8, stride=ROWS), :] = mu[i][:, :128]
    here = lax.axis_index("gx")
    for k in range(GROUP):
        start = 8 * (here ^ k)
        for i in range(Q + 1):
            outs[k][i] = flat[i, pl.ds(pl.multiple_of(start, 8), 8), :]


def finish_kernel(f_ref, r_ref, s_ref, *refs):
    ins, (lam_ref, sens_ref, blocks) = refs[:GROUP], refs[GROUP:]
    here = lax.axis_index("gx")
    for k in range(GROUP):
        blocks[block_of(here ^ k)] = ins[k][...]
    for half in range(2):
        rows = pl.ds(8 * half, 8)
        for layer in range(LAYERS):
            part = slice(4 * layer, 4 * layer + 4)
            tile = [
                jnp.concatenate([blocks[2 * half, i, part, :], blocks[2 * half + 1, i, part, :]], axis=0)
                for i in range(Q + 1)
            ]
            f = [f_ref[i, layer, rows, :] for i in range(Q)]
            out, design = adjoint_lists(tile[:Q], *moments(f), r_ref[layer, rows, :], s_ref[layer, rows, :] == 1)
            for i in range(Q):
                lam_ref[i, layer, rows, :] = out[i]
            sens_ref[layer, rows, :] = tile[Q] + design


def call(kernel, outs, scratch, *args, space=pltpu.VMEM):
    vmem = pl.BlockSpec(memory_space=pltpu.VMEM)
    return pl.pallas_call(
        kernel,
        out_shape=[jax.ShapeDtypeStruct(shape, jnp.float32) for shape in outs],
        in_specs=[pl.BlockSpec(memory_space=space)] * len(args),
        out_specs=[vmem] * len(outs),
        scratch_shapes=[pltpu.VMEM(shape, jnp.float32) if isinstance(shape, tuple) else shape for shape in scratch],
        compiler_params=pltpu.CompilerParams(vmem_limit_bytes=VMEM_LIMIT),
    )(*args)


def ring_pairs(planes, step):
    order = []
    for plane in range(planes):
        for block in range(GROUP):
            gray = (plane - block) % GROUP
            order.append((gray ^ (gray >> 1), plane))
    pairs = []
    for at, (number, plane) in enumerate(order):
        other, beyond = order[(at + step) % len(order)]
        pairs.append((number * planes + plane, other * planes + beyond))
    return pairs


def fast_body(checkpoint, resistance, solid, adjoint_final):
    planes = lax.axis_size("gy")

    def trade(pieces):
        moved = [pieces[0]]
        for k in range(1, GROUP):
            moved.append(lax.ppermute(pieces[k], "gx", [(i, i ^ k) for i in range(GROUP)]))
        return moved

    def swap(value):
        return lax.ppermute(value, "gz", [(0, 1), (1, 0)])

    def ring(up, down):
        lo = lax.ppermute(up, ("gx", "gy"), ring_pairs(planes, 1))
        hi = lax.ppermute(down, ("gx", "gy"), ring_pairs(planes, -1))
        return lo, hi

    given = (checkpoint, resistance, solid, adjoint_final)
    pieces = call(
        send_kernel,
        [(FIELDS, 8, 128)] * GROUP,
        [(GROUP, FIELDS, 8, 128)]
        + [pltpu.VMEM(array.shape, array.dtype) for array in given]
        + [pltpu.SemaphoreType.DMA((len(given),))],
        *[pltpu.with_memory_space_constraint(array, pltpu.HBM) for array in given],
        space=pltpu.HBM,
    )
    pieces = trade(pieces)
    own, up, down = call(
        turn_kernel,
        [(ROWS, FIELDS, 8, 128), (len(FORWARD_UP), 8, 128), (len(FORWARD_DOWN), 8, 128)],
        [(FIELDS, 8 * ROWS, 128)],
        *pieces,
    )
    own_b = swap(own)
    lo, hi = ring(up, down)
    lo_b, hi_b = swap(lo), swap(hi)
    lam, sens, mom1, mom2, rs, up, down = call(
        forward_kernel,
        [
            (ROWS, Q, 8, 256),
            (ROWS, 8, 128),
            (ROWS + 4, 4, 8, 256),
            (ROWS + 4, 4, 8, 256),
            (ROWS + 4, 2, 8, 256),
            (len(BACKWARD_UP) + strip_count(BACKWARD_UP), 8, 128),
            (len(BACKWARD_DOWN) + strip_count(BACKWARD_DOWN), 8, 128),
        ],
        [(ROWS + 6, Q, 8, 256), (ROWS + 4, Q, 8, 256), (ROWS + 2, Q, 8, 256), (ROWS + 2, Q, 8, 256)],
        own,
        own_b,
        lo,
        lo_b,
        hi,
        hi_b,
    )
    lo, hi = ring(up, down)
    pieces = call(
        backward_kernel,
        [(Q + 1, 8, 128)] * GROUP,
        [
            (ROWS + 6, Q, 8, 256),
            (ROWS + 4, Q, 8, 256),
            (ROWS + 4, Q, 8, 256),
            (ROWS + 4, 4, 8, 256),
            (Q + 1, 8 * ROWS, 128),
        ],
        lam,
        sens,
        mom1,
        mom2,
        rs,
        lo,
        hi,
    )
    pieces = trade(pieces)
    return tuple(
        call(
            finish_kernel,
            [checkpoint.shape, resistance.shape],
            [(GROUP, Q + 1, 8, 128)],
            checkpoint,
            resistance,
            solid,
            *pieces,
        )
    )


def padded_2(shard, sides, width):
    for axis, dim in sides:
        count, length = (lax.axis_size(axis), shard.shape[dim])
        up = [(i, (i + 1) % count) for i in range(count)]
        down = [(j, i) for i, j in up]
        last = lax.slice_in_dim(shard, length - width, length, axis=dim)
        leading = lax.slice_in_dim(shard, 0, width, axis=dim)
        before = lax.ppermute(last, axis, up)
        after = lax.ppermute(leading, axis, down)
        shard = jnp.concatenate([before, shard, after], axis=dim)
    return shard


def collide(populations, resistance, solid):
    lattice = jnp.array(VELOCITIES, jnp.float32)
    weights = jnp.array(WEIGHTS, jnp.float32).reshape(-1, 1, 1, 1)
    density = jnp.sum(populations, axis=0)
    momentum = jnp.tensordot(lattice, populations, axes=([0], [0]), precision=lax.Precision.HIGHEST)
    nothing = jnp.zeros_like(density)
    push = jnp.stack([BODY_FORCE * density, nothing, nothing]) - resistance[None] * momentum
    velocity = (momentum + RELAXATION * push) / density[None]
    projected = jnp.tensordot(lattice, velocity, axes=([1], [0]), precision=lax.Precision.HIGHEST)
    speed_squared = jnp.sum(velocity * velocity, axis=0)
    equilibrium = (
        weights
        * density[None]
        * (1.0 + 3.0 * projected + 4.5 * projected * projected - 1.5 * speed_squared[None])
    )
    relaxed = populations - (populations - equilibrium) / RELAXATION
    reflected = jnp.stack([populations[other] for other in OPPOSITE])
    return jnp.where(solid[None] == 1, reflected, relaxed)


def transport(field, sign):
    padded = padded_2(field, (("gx", 1), ("gy", 2), ("gz", 3)), 1)
    first, second, third = (field.shape[1], field.shape[2], field.shape[3])
    pieces = []
    for number, entry in enumerate(VELOCITIES):
        start_a = 1 - sign * entry[0]
        start_b = 1 - sign * entry[1]
        start_c = 1 - sign * entry[2]
        pieces.append(
            padded[
                number,
                start_a : start_a + first,
                start_b : start_b + second,
                start_c : start_c + third,
            ]
        )
    return jnp.stack(pieces)


def general_body(checkpoint, resistance, solid, adjoint_final):
    states = [checkpoint]
    current = checkpoint
    for step in range(STEPS - 1):
        current = transport(collide(current, resistance, solid), 1)
        states.append(current)
    adjoint = adjoint_final
    sensitivity = jnp.zeros_like(resistance)
    for step in reversed(range(STEPS)):
        pulled = transport(adjoint, -1)

        def local_collide(populations, design):
            return collide(populations, design, solid)

        result, backward = jax.vjp(local_collide, states[step], resistance)
        adjoint, design_part = backward(pulled)
        sensitivity = sensitivity + design_part
    return (adjoint, sensitivity)


def body(checkpoint, resistance, solid, adjoint_final):
    fits = (
        lax.axis_size("gx") == GROUP
        and lax.axis_size("gz") == 2
        and resistance.shape == (LAYERS, GROUP * ROWS, 128)
    )
    chosen = fast_body if fits else general_body
    return chosen(checkpoint, resistance, solid, adjoint_final)


def solution(mesh):
    in_specs = (
        P(None, "gx", "gy", "gz"),
        P("gx", "gy", "gz"),
        P("gx", "gy", "gz"),
        P(None, "gx", "gy", "gz"),
    )
    out_specs = (P(None, "gx", "gy", "gz"), P("gx", "gy", "gz"))
    return jax.shard_map(body, mesh=mesh, in_specs=in_specs, out_specs=out_specs, check_vma=False)
```

```python
import functools

import jax
import jax.numpy as jnp
from jax import lax
from jax.experimental import pallas as pl
from jax.experimental.pallas import tpu as pltpu
from jax.sharding import PartitionSpec as P

STEPS = 4


VELOCITIES = (
    (0, 0, 0),
    (1, 0, 0),
    (-1, 0, 0),
    (0, 1, 0),
    (0, -1, 0),
    (0, 0, 1),
    (0, 0, -1),
    (1, 1, 0),
    (-1, -1, 0),
    (1, -1, 0),
    (-1, 1, 0),
    (1, 0, 1),
    (-1, 0, -1),
    (1, 0, -1),
    (-1, 0, 1),
    (0, 1, 1),
    (0, -1, -1),
    (0, 1, -1),
    (0, -1, 1),
)
WEIGHTS = (1.0 / 3.0,) + (1.0 / 18.0,) * 6 + (1.0 / 36.0,) * 12
OPPOSITE = tuple((VELOCITIES.index((-entry[0], -entry[1], -entry[2])) for entry in VELOCITIES))
RELAXATION = 0.8
BODY_FORCE = 0.01

Q = len(VELOCITIES)
KEEP = 1.0 - 1.0 / RELAXATION
PUSH = RELAXATION * BODY_FORCE
VMEM_LIMIT = 16 * 1024 * 1024

GROUP = 4
ROWS = 4
LAYERS = 2
TRADES = (1, 3, 2)
HALO = 3
WIDTH = 2 * HALO
SLOTS = 128 // WIDTH
RES, SOL, ADJ = Q, Q + 1, Q + 2
DOWNWARD = [i for i in range(Q) if VELOCITIES[i][1] > 0]
UPWARD = [i for i in range(Q) if VELOCITIES[i][1] < 0]
EDGES = -(-len(UPWARD) // 2)
FIELDS = ADJ + EDGES

FORWARD_UP = (
    [(3, i, -1) for i in range(Q)]
    + [(2, i, -2) for i in range(Q) if VELOCITIES[i][1] >= 0]
    + [(1, i, -3) for i in range(Q) if VELOCITIES[i][1] > 0]
    + [(3, RES, -1), (3, SOL, -1), (2, RES, -2), (2, SOL, -2)]
    + [(3, ADJ + i, -1) for i in range(Q) if VELOCITIES[i][1] < 0]
)
FORWARD_DOWN = (
    [(0, i, 4) for i in range(Q)]
    + [(1, i, 5) for i in range(Q) if VELOCITIES[i][1] <= 0]
    + [(2, i, 6) for i in range(Q) if VELOCITIES[i][1] < 0]
    + [(0, RES, 4), (0, SOL, 4), (1, RES, 5), (1, SOL, 5)]
    + [(0, ADJ + i, 4) for i in range(Q) if VELOCITIES[i][1] > 0]
)
BACKWARD_UP = (
    [(3, i, -1) for i in range(Q)]
    + [(2, i, -2) for i in range(Q) if VELOCITIES[i][1] <= 0]
    + [(1, i, -3) for i in range(Q) if VELOCITIES[i][1] < 0]
    + [(2, Q + j, -2) for j in range(4)]
)
BACKWARD_DOWN = (
    [(0, i, 4) for i in range(Q)]
    + [(1, i, 5) for i in range(Q) if VELOCITIES[i][1] >= 0]
    + [(2, i, 6) for i in range(Q) if VELOCITIES[i][1] > 0]
    + [(1, Q + j, 5) for j in range(4)]
)


def moments(f):
    plus = [f[i] + f[i + 1] for i in range(1, Q, 2)]
    less = [f[i] - f[i + 1] for i in range(1, Q, 2)]
    density = f[0] + ((plus[0] + plus[1]) + (plus[2] + plus[3])) + ((plus[4] + plus[5]) + (plus[6] + (plus[7] + plus[8])))
    first = less[0] + ((less[3] + less[4]) + (less[5] + less[6]))
    second = less[1] + ((less[3] - less[4]) + (less[7] + less[8]))
    third = less[2] + ((less[5] - less[6]) + (less[7] - less[8]))
    inverse = 1.0 / density
    return density, first * inverse, second * inverse, third * inverse


def strip_count(table):
    return -(-len(table) // SLOTS)


def pack_strips(tiles):
    lane = lax.broadcasted_iota(jnp.int32, (8, 128), 1)
    packed = []
    for number, tile in enumerate(tiles):
        slot = number % SLOTS
        moved = pltpu.roll(tile, (WIDTH * slot + HALO) % 128, axis=1)
        if slot == 0:
            packed.append(moved)
        else:
            packed[-1] = jnp.where(lane >= WIDTH * slot, moved, packed[-1])
    return packed


def unpack_strip(packed, number):
    return pltpu.roll(packed, (-WIDTH * (number % SLOTS) - HALO) % 128, axis=1)


def along(i, x, y, z):
    total = None
    for sign, part in zip(VELOCITIES[i], (x, y, z)):
        if sign == 0:
            continue
        if total is None:
            total = part if sign > 0 else -part
        else:
            total = total + part if sign > 0 else total - part
    return total


def inward(row, last, sign):
    if row == 0:
        return [i for i in range(Q) if sign * VELOCITIES[i][1] > 0]
    if row == last:
        return [i for i in range(Q) if sign * VELOCITIES[i][1] < 0]
    return list(range(Q))


def collide_lists(f, density, vx, vy, vz, resistance, solid):
    damp = 1.0 - RELAXATION * resistance
    ux, uy, uz = damp * vx + PUSH, damp * vy, damp * vz
    base = 1.0 - 1.5 * (ux * ux + uy * uy + uz * uz)
    scaled = {w: density * (w / RELAXATION) for w in sorted(set(WEIGHTS))}
    out = [jnp.where(solid, f[0], KEEP * f[0] + scaled[WEIGHTS[0]] * base)]
    for i in range(1, Q, 2):
        projected = along(i, ux, uy, uz)
        weight = scaled[WEIGHTS[i]]
        even = weight * (base + 4.5 * (projected * projected))
        odd = weight * (3.0 * projected)
        out.append(jnp.where(solid, f[i + 1], KEEP * f[i] + (even + odd)))
        out.append(jnp.where(solid, f[i], KEEP * f[i + 1] + (even - odd)))
    return out


def adjoint_lists(mu, density, vx, vy, vz, resistance, solid):
    damp = 1.0 - RELAXATION * resistance
    ux, uy, uz = damp * vx + PUSH, damp * vy, damp * vz
    plus = [mu[i] + mu[i + 1] for i in range(1, Q, 2)]
    less = [mu[i] - mu[i + 1] for i in range(1, Q, 2)]
    rest, axis, diagonal = (w / RELAXATION for w in (WEIGHTS[0], WEIGHTS[1], WEIGHTS[7]))
    xy, xz, yz = plus[3] + plus[4], plus[5] + plus[6], plus[7] + plus[8]
    zeroth = rest * mu[0] + axis * ((plus[0] + plus[1]) + plus[2]) + diagonal * ((xy + xz) + yz)
    nx = axis * less[0] + diagonal * ((less[3] + less[4]) + (less[5] + less[6]))
    ny = axis * less[1] + diagonal * ((less[3] - less[4]) + (less[7] + less[8]))
    nz = axis * less[2] + diagonal * ((less[5] - less[6]) + (less[7] - less[8]))
    nxx = axis * plus[0] + diagonal * (xy + xz)
    nyy = axis * plus[1] + diagonal * (xy + yz)
    nzz = axis * plus[2] + diagonal * (xz + yz)
    nxy = diagonal * (plus[3] - plus[4])
    nxz = diagonal * (plus[5] - plus[6])
    nyz = diagonal * (plus[7] - plus[8])
    tx = nxx * ux + nxy * uy + nxz * uz
    ty = nxy * ux + nyy * uy + nyz * uz
    tz = nxz * ux + nyz * uy + nzz * uz
    hx = 3.0 * (nx - ux * zeroth) + 9.0 * tx
    hy = 3.0 * (ny - uy * zeroth) + 9.0 * ty
    hz = 3.0 * (nz - uz * zeroth) + 9.0 * tz
    pulled = vx * hx + vy * hy + vz * hz
    square = ux * ux + uy * uy + uz * uz
    scalar = (
        zeroth * (1.0 - 1.5 * square)
        + 3.0 * (nx * ux + ny * uy + nz * uz)
        + 4.5 * (tx * ux + ty * uy + tz * uz)
        - damp * pulled
    )
    qx, qy, qz = damp * hx, damp * hy, damp * hz
    out = [jnp.where(solid, mu[0], KEEP * mu[0] + scalar)]
    for i in range(1, Q, 2):
        slope = along(i, qx, qy, qz)
        out.append(jnp.where(solid, mu[i + 1], KEEP * mu[i] + (scalar + slope)))
        out.append(jnp.where(solid, mu[i], KEEP * mu[i + 1] + (scalar - slope)))
    design = jnp.where(solid, 0.0, (-RELAXATION) * density * pulled)
    return out, design


def shifted(value, i, sign):
    first, _, third = VELOCITIES[i]
    if first:
        value = pltpu.roll(value, (sign * first) % value.shape[0], axis=0)
    if third:
        value = pltpu.roll(value, (sign * third) % value.shape[1], axis=1)
    return value


def block_of(number):
    return (lax.axis_index("gy") + GROUP - (number ^ (number >> 1))) % GROUP


def send_kernel(*refs):
    given, outs, blocks, held, sems = refs[:4], refs[4 : 4 + GROUP], refs[4 + GROUP], refs[5 + GROUP : 9 + GROUP], refs[-1]
    copies = [pltpu.make_async_copy(source, target, sems.at[at]) for at, (source, target) in enumerate(zip(given, held))]
    for copy in copies:
        copy.start()
    for copy in copies[:3]:
        copy.wait()
    f_ref, r_ref, s_ref, a_ref = held
    for half in range(2):
        rows = pl.ds(8 * half, 8)
        tiles = []
        for layer in range(LAYERS):
            f = [f_ref[i, layer, rows, :] for i in range(Q)]
            resistance, kind = r_ref[layer, rows, :], s_ref[layer, rows, :]
            out = collide_lists(f, *moments(f), resistance, kind == 1)
            tiles.append(out + [resistance, kind.astype(jnp.float32)])
        for field in range(ADJ):
            first, second = tiles[0][field], tiles[1][field]
            blocks[2 * half, field] = jnp.concatenate([first[:4], second[:4]], axis=0)
            blocks[2 * half + 1, field] = jnp.concatenate([first[4:], second[4:]], axis=0)
    copies[3].wait()
    for block in range(GROUP):
        for edge in range(EDGES):
            rows = []
            for layer in range(LAYERS):
                for group, row in ((DOWNWARD, 0), (UPWARD, ROWS - 1)):
                    for number in (2 * edge, 2 * edge + 1):
                        i = group[min(number, len(group) - 1)]
                        rows.append(a_ref[i, layer, pl.ds(ROWS * block + row, 1), :])
            blocks[block, ADJ + edge] = jnp.concatenate(rows, axis=0)
    here = lax.axis_index("gx")
    for k in range(GROUP):
        outs[k][...] = blocks[block_of(here ^ k)]


def send_adjoint_kernel(a_hbm, *refs):
    outs, (blocks, a_ref, sem) = refs[:GROUP], refs[GROUP:]
    copy = pltpu.make_async_copy(a_hbm, a_ref, sem)
    copy.start()
    copy.wait()
    for block in range(GROUP):
        for i in range(Q):
            blocks[block, i] = jnp.concatenate([a_ref[i, layer, pl.ds(4 * block, 4), :] for layer in range(LAYERS)], axis=0)
    here = lax.axis_index("gx")
    for k in range(GROUP):
        outs[k][...] = blocks[block_of(here ^ k)]


def gather_pieces(ins, flat):
    here = lax.axis_index("gx")
    for k in range(GROUP):
        start = 8 * (here ^ k)
        for field in range(flat.shape[0]):
            flat[field, pl.ds(pl.multiple_of(start, 8), 8), :] = ins[k][field]


def turn_kernel(*refs):
    ins, (own, up, down, flat) = refs[:GROUP], refs[GROUP:]
    gather_pieces(ins, flat)
    for field in range(ADJ):
        for row in range(ROWS):
            own[row, field] = flat[field, pl.ds(row, 8, stride=ROWS), :]
    for table, part in ((FORWARD_UP, up), (FORWARD_DOWN, down)):
        for number, (row, field, _) in enumerate(table):
            if field < ADJ:
                part[number] = own[row, field]
            else:
                group, base = (UPWARD, 2) if row else (DOWNWARD, 0)
                edge, slot = divmod(group.index(field - ADJ), 2)
                part[number] = flat[ADJ + edge, pl.ds(base + slot, 8, stride=ROWS), :]


def turn_adjoint_kernel(*refs):
    ins, (own, flat) = refs[:GROUP], refs[GROUP:]
    gather_pieces(ins, flat)
    for field in range(Q):
        for row in range(ROWS):
            own[row, field] = flat[field, pl.ds(row, 8, stride=ROWS), :]


def forward_kernel(own_a, own_b, adj_a, adj_b, lo_a, lo_b, hi_a, hi_b, lam_ref, sens_ref, mom1, mom2, rs_ref, up, down, p0, p1, p2, a4):
    for side, own, adj in ((0, own_a, adj_a), (1, own_b, adj_b)):
        lanes = slice(128 * side, 128 * side + 128)
        for row in range(ROWS):
            for i in range(Q):
                p0[row + 3, i, :, lanes] = own[row, i]
                a4[row + 1, i, :, lanes] = adj[row, i]
            for j in range(2):
                rs_ref[row + 2, j, :, lanes] = own[row, RES + j]
    for table, parts in ((FORWARD_UP, (lo_a, lo_b)), (FORWARD_DOWN, (hi_a, hi_b))):
        for side, part in enumerate(parts):
            lanes = slice(128 * side, 128 * side + 128)
            for number, (_, field, row) in enumerate(table):
                if field < Q:
                    p0[row + 3, field, :, lanes] = part[number]
                elif field < ADJ:
                    rs_ref[row + 2, field - RES, :, lanes] = part[number]
                else:
                    a4[row + 1, field - ADJ, :, lanes] = part[number]

    def pull(source, row):
        return [shifted(source[row + 1 - VELOCITIES[i][1], i], i, 1) for i in range(Q)]

    def first(row):
        f = pull(p0, row)
        moment = moments(f)
        for j in range(4):
            mom1[row, j] = moment[j]
        out = collide_lists(f, *moment, rs_ref[row, 0], rs_ref[row, 1] == 1.0)
        for i in inward(row, ROWS + 3, 1):
            p1[row, i] = out[i]

    for row in range(ROWS + 4):
        first(row)

    def second(row):
        f = pull(p1, row)
        moment = moments(f)
        for j in range(4):
            mom2[row + 1, j] = moment[j]
        out = collide_lists(f, *moment, rs_ref[row + 1, 0], rs_ref[row + 1, 1] == 1.0)
        for i in inward(row, ROWS + 1, 1):
            p2[row, i] = out[i]

    for row in range(ROWS + 2):
        second(row)

    def third(row):
        moment = moments(pull(p2, row))
        mu = [shifted(a4[row + 1 + VELOCITIES[i][1], i], i, -1) for i in range(Q)]
        out, design = adjoint_lists(mu, *moment, rs_ref[row + 2, 0], rs_ref[row + 2, 1] == 1.0)
        for i in range(Q):
            lam_ref[row, i] = out[i]
        sens_ref[row] = design[:, :128]

    for row in range(ROWS):
        third(row)
    for table, part in ((BACKWARD_UP, up), (BACKWARD_DOWN, down)):
        others = []
        for number, (row, field, _) in enumerate(table):
            source = lam_ref[row, field] if field < Q else mom2[row + 2, field - Q]
            part[number] = source[:, :128]
            others.append(source[:, 128:])
        for number, tile in enumerate(pack_strips(others)):
            part[len(table) + number] = tile
    for row in (0, ROWS + 3):
        for j in range(4):
            mom2[row, j] = jnp.zeros((8, 256), jnp.float32)


def backward_kernel(lam_ref, sens_ref, mom1, mom2, rs_ref, lo, hi, *refs):
    outs, (l3, l2, l1, m2, flat) = refs[:GROUP], refs[GROUP:]
    for row in range(ROWS):
        for i in range(Q):
            l3[row + 3, i] = lam_ref[row, i]
    for row in range(ROWS + 4):
        for j in range(4):
            m2[row, j] = mom2[row, j]
    for table, part in ((BACKWARD_UP, lo), (BACKWARD_DOWN, hi)):
        packed = [part[len(table) + number] for number in range(strip_count(table))]
        for number, (_, field, row) in enumerate(table):
            target = l3.at[row + 3, field] if field < Q else m2.at[row + 2, field - Q]
            target[:, :128] = part[number]
            target[:, 128:] = unpack_strip(packed[number // SLOTS], number)

    def pull(source, row):
        return [shifted(source[row + 1 + VELOCITIES[i][1], i], i, -1) for i in range(Q)]

    designs = {}

    def second(row):
        mu = pull(l3, row)
        out, design = adjoint_lists(mu, *[m2[row, j] for j in range(4)], rs_ref[row, 0], rs_ref[row, 1] == 1.0)
        for i in inward(row, ROWS + 3, -1):
            l2[row, i] = out[i]
        if 2 <= row < ROWS + 2:
            designs[row - 2] = design

    for row in range(ROWS + 4):
        second(row)

    def first(row):
        mu = pull(l2, row)
        out, design = adjoint_lists(
            mu, *[mom1[row + 1, j] for j in range(4)], rs_ref[row + 1, 0], rs_ref[row + 1, 1] == 1.0
        )
        for i in inward(row, ROWS + 1, -1):
            l1[row, i] = out[i]
        if 1 <= row < ROWS + 1:
            designs[row - 1] = designs[row - 1] + design

    for row in range(ROWS + 2):
        first(row)
    for row in range(ROWS):
        flat[Q, pl.ds(row, 8, stride=ROWS), :] = sens_ref[row] + designs[row][:, :128]
        mu = pull(l1, row)
        for i in range(Q):
            flat[i, pl.ds(row, 8, stride=ROWS), :] = mu[i][:, :128]
    here = lax.axis_index("gx")
    for k in range(GROUP):
        start = 8 * (here ^ k)
        for i in range(Q + 1):
            outs[k][i] = flat[i, pl.ds(pl.multiple_of(start, 8), 8), :]


def finish_kernel(f_ref, r_ref, s_ref, *refs):
    ins, (lam_ref, sens_ref, blocks) = refs[:GROUP], refs[GROUP:]
    here = lax.axis_index("gx")
    for k in range(GROUP):
        blocks[block_of(here ^ k)] = ins[k][...]
    for half in range(2):
        rows = pl.ds(8 * half, 8)
        for layer in range(LAYERS):
            part = slice(4 * layer, 4 * layer + 4)
            tile = [
                jnp.concatenate([blocks[2 * half, i, part, :], blocks[2 * half + 1, i, part, :]], axis=0)
                for i in range(Q + 1)
            ]
            f = [f_ref[i, layer, rows, :] for i in range(Q)]
            out, design = adjoint_lists(tile[:Q], *moments(f), r_ref[layer, rows, :], s_ref[layer, rows, :] == 1)
            for i in range(Q):
                lam_ref[i, layer, rows, :] = out[i]
            sens_ref[layer, rows, :] = tile[Q] + design


def call(kernel, outs, scratch, *args, space=pltpu.VMEM):
    vmem = pl.BlockSpec(memory_space=pltpu.VMEM)
    return pl.pallas_call(
        kernel,
        out_shape=[jax.ShapeDtypeStruct(shape, jnp.float32) for shape in outs],
        in_specs=[pl.BlockSpec(memory_space=space)] * len(args),
        out_specs=[vmem] * len(outs),
        scratch_shapes=[pltpu.VMEM(shape, jnp.float32) if isinstance(shape, tuple) else shape for shape in scratch],
        compiler_params=pltpu.CompilerParams(vmem_limit_bytes=VMEM_LIMIT),
    )(*args)


def ring_pairs(planes, step):
    order = []
    for plane in range(planes):
        for block in range(GROUP):
            gray = (plane - block) % GROUP
            order.append((gray ^ (gray >> 1)) * planes + plane)
    return [(here, order[(at + step) % len(order)]) for at, here in enumerate(order)]


def fast_body(checkpoint, resistance, solid, adjoint_final):
    planes = lax.axis_size("gy")

    def trade(pieces):
        moved = list(pieces)
        for k in TRADES:
            moved[k] = lax.ppermute(pieces[k], "gx", [(i, i ^ k) for i in range(GROUP)])
        return moved

    def swap(value):
        return lax.ppermute(value, "gz", [(0, 1), (1, 0)])

    def ring(up, down):
        lo = lax.ppermute(up, ("gx", "gy"), ring_pairs(planes, 1))
        hi = lax.ppermute(down, ("gx", "gy"), ring_pairs(planes, -1))
        return lo, hi

    given = (checkpoint, resistance, solid, adjoint_final)
    pieces = call(
        send_kernel,
        [(FIELDS, 8, 128)] * GROUP,
        [(GROUP, FIELDS, 8, 128)]
        + [pltpu.VMEM(array.shape, array.dtype) for array in given]
        + [pltpu.SemaphoreType.DMA((len(given),))],
        *[pltpu.with_memory_space_constraint(array, pltpu.HBM) for array in given],
        space=pltpu.HBM,
    )
    fenced = lax.optimization_barrier((adjoint_final, *pieces))
    adjoint_pieces = call(
        send_adjoint_kernel,
        [(Q, 8, 128)] * GROUP,
        [(GROUP, Q, 8, 128), pltpu.VMEM(adjoint_final.shape, jnp.float32), pltpu.SemaphoreType.DMA],
        pltpu.with_memory_space_constraint(fenced[0], pltpu.HBM),
        space=pltpu.HBM,
    )
    pieces = trade(fenced[1:])
    own, up, down = call(
        turn_kernel,
        [(ROWS, ADJ, 8, 128), (len(FORWARD_UP), 8, 128), (len(FORWARD_DOWN), 8, 128)],
        [(FIELDS, 8 * ROWS, 128)],
        *pieces,
    )
    own_b = swap(own)
    (adj,) = call(turn_adjoint_kernel, [(ROWS, Q, 8, 128)], [(Q, 8 * ROWS, 128)], *trade(adjoint_pieces))
    adj_b = swap(adj)
    lo, hi = ring(up, down)
    lo_b, hi_b = swap(lo), swap(hi)
    lam, sens, mom1, mom2, rs, up, down = call(
        forward_kernel,
        [
            (ROWS, Q, 8, 256),
            (ROWS, 8, 128),
            (ROWS + 4, 4, 8, 256),
            (ROWS + 4, 4, 8, 256),
            (ROWS + 4, 2, 8, 256),
            (len(BACKWARD_UP) + strip_count(BACKWARD_UP), 8, 128),
            (len(BACKWARD_DOWN) + strip_count(BACKWARD_DOWN), 8, 128),
        ],
        [(ROWS + 6, Q, 8, 256), (ROWS + 4, Q, 8, 256), (ROWS + 2, Q, 8, 256), (ROWS + 2, Q, 8, 256)],
        own,
        own_b,
        adj,
        adj_b,
        lo,
        lo_b,
        hi,
        hi_b,
    )
    lo, hi = ring(up, down)
    pieces = call(
        backward_kernel,
        [(Q + 1, 8, 128)] * GROUP,
        [
            (ROWS + 6, Q, 8, 256),
            (ROWS + 4, Q, 8, 256),
            (ROWS + 4, Q, 8, 256),
            (ROWS + 4, 4, 8, 256),
            (Q + 1, 8 * ROWS, 128),
        ],
        lam,
        sens,
        mom1,
        mom2,
        rs,
        lo,
        hi,
    )
    pieces = trade(pieces)
    return tuple(
        call(
            finish_kernel,
            [checkpoint.shape, resistance.shape],
            [(GROUP, Q + 1, 8, 128)],
            checkpoint,
            resistance,
            solid,
            *pieces,
        )
    )


def padded_2(shard, sides, width):
    for axis, dim in sides:
        count, length = (lax.axis_size(axis), shard.shape[dim])
        up = [(i, (i + 1) % count) for i in range(count)]
        down = [(j, i) for i, j in up]
        last = lax.slice_in_dim(shard, length - width, length, axis=dim)
        leading = lax.slice_in_dim(shard, 0, width, axis=dim)
        before = lax.ppermute(last, axis, up)
        after = lax.ppermute(leading, axis, down)
        shard = jnp.concatenate([before, shard, after], axis=dim)
    return shard


def collide(populations, resistance, solid):
    lattice = jnp.array(VELOCITIES, jnp.float32)
    weights = jnp.array(WEIGHTS, jnp.float32).reshape(-1, 1, 1, 1)
    density = jnp.sum(populations, axis=0)
    momentum = jnp.tensordot(lattice, populations, axes=([0], [0]), precision=lax.Precision.HIGHEST)
    nothing = jnp.zeros_like(density)
    push = jnp.stack([BODY_FORCE * density, nothing, nothing]) - resistance[None] * momentum
    velocity = (momentum + RELAXATION * push) / density[None]
    projected = jnp.tensordot(lattice, velocity, axes=([1], [0]), precision=lax.Precision.HIGHEST)
    speed_squared = jnp.sum(velocity * velocity, axis=0)
    equilibrium = (
        weights
        * density[None]
        * (1.0 + 3.0 * projected + 4.5 * projected * projected - 1.5 * speed_squared[None])
    )
    relaxed = populations - (populations - equilibrium) / RELAXATION
    reflected = jnp.stack([populations[other] for other in OPPOSITE])
    return jnp.where(solid[None] == 1, reflected, relaxed)


def transport(field, sign):
    padded = padded_2(field, (("gx", 1), ("gy", 2), ("gz", 3)), 1)
    first, second, third = (field.shape[1], field.shape[2], field.shape[3])
    pieces = []
    for number, entry in enumerate(VELOCITIES):
        start_a = 1 - sign * entry[0]
        start_b = 1 - sign * entry[1]
        start_c = 1 - sign * entry[2]
        pieces.append(
            padded[
                number,
                start_a : start_a + first,
                start_b : start_b + second,
                start_c : start_c + third,
            ]
        )
    return jnp.stack(pieces)


def general_body(checkpoint, resistance, solid, adjoint_final):
    states = [checkpoint]
    current = checkpoint
    for step in range(STEPS - 1):
        current = transport(collide(current, resistance, solid), 1)
        states.append(current)
    adjoint = adjoint_final
    sensitivity = jnp.zeros_like(resistance)
    for step in reversed(range(STEPS)):
        pulled = transport(adjoint, -1)

        def local_collide(populations, design):
            return collide(populations, design, solid)

        result, backward = jax.vjp(local_collide, states[step], resistance)
        adjoint, design_part = backward(pulled)
        sensitivity = sensitivity + design_part
    return (adjoint, sensitivity)


def body(checkpoint, resistance, solid, adjoint_final):
    fits = (
        lax.axis_size("gx") == GROUP
        and lax.axis_size("gz") == 2
        and resistance.shape == (LAYERS, GROUP * ROWS, 128)
    )
    chosen = fast_body if fits else general_body
    return chosen(checkpoint, resistance, solid, adjoint_final)


def solution(mesh):
    in_specs = (
        P(None, "gx", "gy", "gz"),
        P("gx", "gy", "gz"),
        P("gx", "gy", "gz"),
        P(None, "gx", "gy", "gz"),
    )
    out_specs = (P(None, "gx", "gy", "gz"), P("gx", "gy", "gz"))
    return jax.shard_map(body, mesh=mesh, in_specs=in_specs, out_specs=out_specs, check_vma=False)
```

```python
import functools

import jax
import jax.numpy as jnp
from jax import lax
from jax.experimental import pallas as pl
from jax.experimental.pallas import tpu as pltpu
from jax.sharding import PartitionSpec as P

STEPS = 4


VELOCITIES = (
    (0, 0, 0),
    (1, 0, 0),
    (-1, 0, 0),
    (0, 1, 0),
    (0, -1, 0),
    (0, 0, 1),
    (0, 0, -1),
    (1, 1, 0),
    (-1, -1, 0),
    (1, -1, 0),
    (-1, 1, 0),
    (1, 0, 1),
    (-1, 0, -1),
    (1, 0, -1),
    (-1, 0, 1),
    (0, 1, 1),
    (0, -1, -1),
    (0, 1, -1),
    (0, -1, 1),
)
WEIGHTS = (1.0 / 3.0,) + (1.0 / 18.0,) * 6 + (1.0 / 36.0,) * 12
OPPOSITE = tuple((VELOCITIES.index((-entry[0], -entry[1], -entry[2])) for entry in VELOCITIES))
RELAXATION = 0.8
BODY_FORCE = 0.01

Q = len(VELOCITIES)
KEEP = 1.0 - 1.0 / RELAXATION
PUSH = RELAXATION * BODY_FORCE
VMEM_LIMIT = 16 * 1024 * 1024

GROUP = 4
ROWS = 4
LAYERS = 2
TRADES = (1, 3, 2)
FORWARD_REACH, BACKWARD_REACH = 6, 3
RES, SOL, ADJ = Q, Q + 1, Q + 2
DOWNWARD = [i for i in range(Q) if VELOCITIES[i][1] > 0]
UPWARD = [i for i in range(Q) if VELOCITIES[i][1] < 0]
EDGES = -(-len(UPWARD) // 2)
FIELDS = ADJ + EDGES

FORWARD_UP = (
    [(3, i, -1) for i in range(Q)]
    + [(2, i, -2) for i in range(Q) if VELOCITIES[i][1] >= 0]
    + [(1, i, -3) for i in range(Q) if VELOCITIES[i][1] > 0]
    + [(3, RES, -1), (3, SOL, -1), (2, RES, -2), (2, SOL, -2)]
    + [(3, ADJ + i, -1) for i in range(Q) if VELOCITIES[i][1] < 0]
)
FORWARD_DOWN = (
    [(0, i, 4) for i in range(Q)]
    + [(1, i, 5) for i in range(Q) if VELOCITIES[i][1] <= 0]
    + [(2, i, 6) for i in range(Q) if VELOCITIES[i][1] < 0]
    + [(0, RES, 4), (0, SOL, 4), (1, RES, 5), (1, SOL, 5)]
    + [(0, ADJ + i, 4) for i in range(Q) if VELOCITIES[i][1] > 0]
)
OWN = [(row, field) for row in range(ROWS) for field in range(ADJ)]
OWN_ADJOINT = [(row, field) for row in range(ROWS) for field in range(Q)]
BACKWARD_UP = (
    [(3, i, -1) for i in range(Q)]
    + [(2, i, -2) for i in range(Q) if VELOCITIES[i][1] <= 0]
    + [(1, i, -3) for i in range(Q) if VELOCITIES[i][1] < 0]
    + [(2, Q + j, -2) for j in range(4)]
)
BACKWARD_DOWN = (
    [(0, i, 4) for i in range(Q)]
    + [(1, i, 5) for i in range(Q) if VELOCITIES[i][1] >= 0]
    + [(2, i, 6) for i in range(Q) if VELOCITIES[i][1] > 0]
    + [(1, Q + j, 5) for j in range(4)]
)


def moments(f):
    plus = [f[i] + f[i + 1] for i in range(1, Q, 2)]
    less = [f[i] - f[i + 1] for i in range(1, Q, 2)]
    density = f[0] + ((plus[0] + plus[1]) + (plus[2] + plus[3])) + ((plus[4] + plus[5]) + (plus[6] + (plus[7] + plus[8])))
    first = less[0] + ((less[3] + less[4]) + (less[5] + less[6]))
    second = less[1] + ((less[3] - less[4]) + (less[7] + less[8]))
    third = less[2] + ((less[5] - less[6]) + (less[7] - less[8]))
    inverse = 1.0 / density
    return density, first * inverse, second * inverse, third * inverse


def slots_of(reach):
    return 128 // (2 * reach)


def strip_count(table, reach):
    return -(-len(table) // slots_of(reach))


def pack_strips(tiles, reach):
    lane = lax.broadcasted_iota(jnp.int32, (8, 128), 1)
    packed = []
    for number, tile in enumerate(tiles):
        start = 2 * reach * (number % slots_of(reach))
        moved = pltpu.roll(tile, start + reach, axis=1)
        if start == 0:
            packed.append(moved)
        else:
            packed[-1] = jnp.where(lane >= start, moved, packed[-1])
    return packed


def unpack_strip(packed, number, reach):
    start = 2 * reach * (number % slots_of(reach))
    return pltpu.roll(packed[number // slots_of(reach)], 128 - start - reach, axis=1)


def along(i, x, y, z):
    total = None
    for sign, part in zip(VELOCITIES[i], (x, y, z)):
        if sign == 0:
            continue
        if total is None:
            total = part if sign > 0 else -part
        else:
            total = total + part if sign > 0 else total - part
    return total


def inward(row, last, sign):
    if row == 0:
        return [i for i in range(Q) if sign * VELOCITIES[i][1] > 0]
    if row == last:
        return [i for i in range(Q) if sign * VELOCITIES[i][1] < 0]
    return list(range(Q))


def collide_lists(f, density, vx, vy, vz, resistance, solid):
    damp = 1.0 - RELAXATION * resistance
    ux, uy, uz = damp * vx + PUSH, damp * vy, damp * vz
    base = 1.0 - 1.5 * (ux * ux + uy * uy + uz * uz)
    scaled = {w: density * (w / RELAXATION) for w in sorted(set(WEIGHTS))}
    out = [jnp.where(solid, f[0], KEEP * f[0] + scaled[WEIGHTS[0]] * base)]
    for i in range(1, Q, 2):
        projected = along(i, ux, uy, uz)
        weight = scaled[WEIGHTS[i]]
        even = weight * (base + 4.5 * (projected * projected))
        odd = weight * (3.0 * projected)
        out.append(jnp.where(solid, f[i + 1], KEEP * f[i] + (even + odd)))
        out.append(jnp.where(solid, f[i], KEEP * f[i + 1] + (even - odd)))
    return out


def adjoint_lists(mu, density, vx, vy, vz, resistance, solid):
    damp = 1.0 - RELAXATION * resistance
    ux, uy, uz = damp * vx + PUSH, damp * vy, damp * vz
    plus = [mu[i] + mu[i + 1] for i in range(1, Q, 2)]
    less = [mu[i] - mu[i + 1] for i in range(1, Q, 2)]
    rest, axis, diagonal = (w / RELAXATION for w in (WEIGHTS[0], WEIGHTS[1], WEIGHTS[7]))
    xy, xz, yz = plus[3] + plus[4], plus[5] + plus[6], plus[7] + plus[8]
    zeroth = rest * mu[0] + axis * ((plus[0] + plus[1]) + plus[2]) + diagonal * ((xy + xz) + yz)
    nx = axis * less[0] + diagonal * ((less[3] + less[4]) + (less[5] + less[6]))
    ny = axis * less[1] + diagonal * ((less[3] - less[4]) + (less[7] + less[8]))
    nz = axis * less[2] + diagonal * ((less[5] - less[6]) + (less[7] - less[8]))
    nxx = axis * plus[0] + diagonal * (xy + xz)
    nyy = axis * plus[1] + diagonal * (xy + yz)
    nzz = axis * plus[2] + diagonal * (xz + yz)
    nxy = diagonal * (plus[3] - plus[4])
    nxz = diagonal * (plus[5] - plus[6])
    nyz = diagonal * (plus[7] - plus[8])
    tx = nxx * ux + nxy * uy + nxz * uz
    ty = nxy * ux + nyy * uy + nyz * uz
    tz = nxz * ux + nyz * uy + nzz * uz
    hx = 3.0 * (nx - ux * zeroth) + 9.0 * tx
    hy = 3.0 * (ny - uy * zeroth) + 9.0 * ty
    hz = 3.0 * (nz - uz * zeroth) + 9.0 * tz
    pulled = vx * hx + vy * hy + vz * hz
    square = ux * ux + uy * uy + uz * uz
    scalar = (
        zeroth * (1.0 - 1.5 * square)
        + 3.0 * (nx * ux + ny * uy + nz * uz)
        + 4.5 * (tx * ux + ty * uy + tz * uz)
        - damp * pulled
    )
    qx, qy, qz = damp * hx, damp * hy, damp * hz
    out = [jnp.where(solid, mu[0], KEEP * mu[0] + scalar)]
    for i in range(1, Q, 2):
        slope = along(i, qx, qy, qz)
        out.append(jnp.where(solid, mu[i + 1], KEEP * mu[i] + (scalar + slope)))
        out.append(jnp.where(solid, mu[i], KEEP * mu[i + 1] + (scalar - slope)))
    design = jnp.where(solid, 0.0, (-RELAXATION) * density * pulled)
    return out, design


def shifted(value, i, sign):
    first, _, third = VELOCITIES[i]
    if first:
        value = pltpu.roll(value, (sign * first) % value.shape[0], axis=0)
    if third:
        value = pltpu.roll(value, (sign * third) % value.shape[1], axis=1)
    return value


def block_of(number):
    return (lax.axis_index("gy") + GROUP - (number ^ (number >> 1))) % GROUP


def send_kernel(*refs):
    given, outs, blocks, held, sems = refs[:4], refs[4 : 4 + GROUP], refs[4 + GROUP], refs[5 + GROUP : 9 + GROUP], refs[-1]
    copies = [pltpu.make_async_copy(source, target, sems.at[at]) for at, (source, target) in enumerate(zip(given, held))]
    for copy in copies:
        copy.start()
    for copy in copies[:3]:
        copy.wait()
    f_ref, r_ref, s_ref, a_ref = held
    for half in range(2):
        rows = pl.ds(8 * half, 8)
        tiles = []
        for layer in range(LAYERS):
            f = [f_ref[i, layer, rows, :] for i in range(Q)]
            resistance, kind = r_ref[layer, rows, :], s_ref[layer, rows, :]
            out = collide_lists(f, *moments(f), resistance, kind == 1)
            tiles.append(out + [resistance, kind.astype(jnp.float32)])
        for field in range(ADJ):
            first, second = tiles[0][field], tiles[1][field]
            blocks[2 * half, field] = jnp.concatenate([first[:4], second[:4]], axis=0)
            blocks[2 * half + 1, field] = jnp.concatenate([first[4:], second[4:]], axis=0)
    copies[3].wait()
    for block in range(GROUP):
        for edge in range(EDGES):
            rows = []
            for layer in range(LAYERS):
                for group, row in ((DOWNWARD, 0), (UPWARD, ROWS - 1)):
                    for number in (2 * edge, 2 * edge + 1):
                        i = group[min(number, len(group) - 1)]
                        rows.append(a_ref[i, layer, pl.ds(ROWS * block + row, 1), :])
            blocks[block, ADJ + edge] = jnp.concatenate(rows, axis=0)
    here = lax.axis_index("gx")
    for k in range(GROUP):
        outs[k][...] = blocks[block_of(here ^ k)]


def send_adjoint_kernel(a_hbm, *refs):
    outs, (blocks, a_ref, sem) = refs[:GROUP], refs[GROUP:]
    copy = pltpu.make_async_copy(a_hbm, a_ref, sem)
    copy.start()
    copy.wait()
    for block in range(GROUP):
        for i in range(Q):
            blocks[block, i] = jnp.concatenate([a_ref[i, layer, pl.ds(4 * block, 4), :] for layer in range(LAYERS)], axis=0)
    here = lax.axis_index("gx")
    for k in range(GROUP):
        outs[k][...] = blocks[block_of(here ^ k)]


def gather_pieces(ins, flat):
    here = lax.axis_index("gx")
    for k in range(GROUP):
        start = 8 * (here ^ k)
        for field in range(flat.shape[0]):
            flat[field, pl.ds(pl.multiple_of(start, 8), 8), :] = ins[k][field]


def turn_kernel(*refs):
    ins, (own, up, down, flat) = refs[:GROUP], refs[GROUP:]
    gather_pieces(ins, flat)
    for field in range(ADJ):
        for row in range(ROWS):
            own[row, field] = flat[field, pl.ds(row, 8, stride=ROWS), :]
    for table, part in ((FORWARD_UP, up), (FORWARD_DOWN, down)):
        for number, (row, field, _) in enumerate(table):
            if field < ADJ:
                part[number] = own[row, field]
            else:
                group, base = (UPWARD, 2) if row else (DOWNWARD, 0)
                edge, slot = divmod(group.index(field - ADJ), 2)
                part[number] = flat[ADJ + edge, pl.ds(base + slot, 8, stride=ROWS), :]


def turn_adjoint_kernel(*refs):
    ins, (adj, flat) = refs[:GROUP], refs[GROUP:]
    gather_pieces(ins, flat)
    for field in range(Q):
        for row in range(ROWS):
            adj[row, field] = flat[field, pl.ds(row, 8, stride=ROWS), :]


def stream_pull(source, row, sign):
    return [shifted(source[row + 1 - sign * VELOCITIES[i][1], i], i, sign) for i in range(Q)]


def place(target, own_half, packed, number, reach):
    target[:, :128] = own_half
    target[:, 128:] = unpack_strip(packed, number, reach)


def forward_kernel(
    own_a, own_b, adj_a, adj_b, lo_a, lo_b, hi_a, hi_b, lam_ref, sens_ref, mom1, mom2, rs_ref, up, down, p0, p1, p2, a4
):
    def target(field, row):
        if field < Q:
            return p0.at[row + 3, field]
        return rs_ref.at[row + 2, field - RES] if field < ADJ else a4.at[row + 1, field - ADJ]

    for side, own, adj in ((0, own_a, adj_a), (1, own_b, adj_b)):
        lanes = slice(128 * side, 128 * side + 128)
        for row, field in OWN:
            target(field, row)[:, lanes] = own[row, field]
        for row, field in OWN_ADJOINT:
            target(ADJ + field, row)[:, lanes] = adj[row, field]
    for table, parts in ((FORWARD_UP, (lo_a, lo_b)), (FORWARD_DOWN, (hi_a, hi_b))):
        for side, part in enumerate(parts):
            for number, (_, field, row) in enumerate(table):
                target(field, row)[:, slice(128 * side, 128 * side + 128)] = part[number]
    for row in range(ROWS + 4):
        f = stream_pull(p0, row, 1)
        moment = moments(f)
        for j in range(4):
            mom1[row, j] = moment[j]
        out = collide_lists(f, *moment, rs_ref[row, 0], rs_ref[row, 1] == 1.0)
        for i in inward(row, ROWS + 3, 1):
            p1[row, i] = out[i]
    for row in range(ROWS + 2):
        f = stream_pull(p1, row, 1)
        moment = moments(f)
        for j in range(4):
            mom2[row, j] = moment[j]
        out = collide_lists(f, *moment, rs_ref[row + 1, 0], rs_ref[row + 1, 1] == 1.0)
        for i in inward(row, ROWS + 1, 1):
            p2[row, i] = out[i]
    for row in range(ROWS):
        moment = moments(stream_pull(p2, row, 1))
        mu = stream_pull(a4, row, -1)
        out, design = adjoint_lists(mu, *moment, rs_ref[row + 2, 0], rs_ref[row + 2, 1] == 1.0)
        for i in range(Q):
            lam_ref[row, i] = out[i]
        sens_ref[row] = design[:, :128]
    for table, part in ((BACKWARD_UP, up), (BACKWARD_DOWN, down)):
        others = []
        for number, (row, field, _) in enumerate(table):
            source = lam_ref[row, field] if field < Q else mom2[row + 1, field - Q]
            part[number] = source[:, :128]
            others.append(source[:, 128:])
        for number, tile in enumerate(pack_strips(others, BACKWARD_REACH)):
            part[len(table) + number] = tile


def inner_backward_kernel(lam_ref, sens_ref, mom2, rs_ref, l2, sens_out):
    for row in (0, ROWS - 1):
        sens_out[row] = sens_ref[row]
    for row in range(ROWS - 2):
        mu = stream_pull(lam_ref, row, -1)
        moment = [mom2[row + 2, j] for j in range(4)]
        out, design = adjoint_lists(mu, *moment, rs_ref[row + 3, 0], rs_ref[row + 3, 1] == 1.0)
        for i in range(Q):
            l2[row, i] = out[i]
        sens_out[row + 1] = sens_ref[row + 1] + design[:, :128]


def backward_kernel(lam_ref, sens_ref, mom1, mom2, rs_ref, l2_inner, lo, hi, *refs):
    outs, (l3, l2, l1, m2, flat) = refs[:GROUP], refs[GROUP:]
    for row in range(ROWS):
        for i in range(Q):
            l3[row + 3, i] = lam_ref[row, i]
    for row in range(ROWS + 2):
        for j in range(4):
            m2[row + 1, j] = mom2[row, j]
    for table, part in ((BACKWARD_UP, lo), (BACKWARD_DOWN, hi)):
        packed = [part[len(table) + number] for number in range(strip_count(table, BACKWARD_REACH))]
        for number, (_, field, row) in enumerate(table):
            target = l3.at[row + 3, field] if field < Q else m2.at[row + 2, field - Q]
            place(target, part[number], packed, number, BACKWARD_REACH)
    designs = [sens_ref[row] for row in range(ROWS)]
    for row in range(ROWS + 4):
        if 3 <= row < ROWS + 1:
            for i in range(Q):
                l2[row, i] = l2_inner[row - 3, i]
            continue
        mu = stream_pull(l3, row, -1)
        out, design = adjoint_lists(mu, *[m2[row, j] for j in range(4)], rs_ref[row, 0], rs_ref[row, 1] == 1.0)
        for i in inward(row, ROWS + 3, -1):
            l2[row, i] = out[i]
        if 2 <= row < ROWS + 2:
            designs[row - 2] = designs[row - 2] + design[:, :128]
    for row in range(ROWS + 2):
        mu = stream_pull(l2, row, -1)
        moment = [mom1[row + 1, j] for j in range(4)]
        out, design = adjoint_lists(mu, *moment, rs_ref[row + 1, 0], rs_ref[row + 1, 1] == 1.0)
        for i in inward(row, ROWS + 1, -1):
            l1[row, i] = out[i]
        if 1 <= row < ROWS + 1:
            designs[row - 1] = designs[row - 1] + design[:, :128]
    for row in range(ROWS):
        flat[Q, pl.ds(row, 8, stride=ROWS), :] = designs[row]
        mu = stream_pull(l1, row, -1)
        for i in range(Q):
            flat[i, pl.ds(row, 8, stride=ROWS), :] = mu[i][:, :128]
    here = lax.axis_index("gx")
    for k in range(GROUP):
        start = 8 * (here ^ k)
        for i in range(Q + 1):
            outs[k][i] = flat[i, pl.ds(pl.multiple_of(start, 8), 8), :]


def finish_kernel(f_ref, r_ref, s_ref, *refs):
    ins, (lam_ref, sens_ref, blocks) = refs[:GROUP], refs[GROUP:]
    here = lax.axis_index("gx")
    for k in range(GROUP):
        blocks[block_of(here ^ k)] = ins[k][...]
    for half in range(2):
        rows = pl.ds(8 * half, 8)
        for layer in range(LAYERS):
            part = slice(4 * layer, 4 * layer + 4)
            tile = [
                jnp.concatenate([blocks[2 * half, i, part, :], blocks[2 * half + 1, i, part, :]], axis=0)
                for i in range(Q + 1)
            ]
            f = [f_ref[i, layer, rows, :] for i in range(Q)]
            out, design = adjoint_lists(tile[:Q], *moments(f), r_ref[layer, rows, :], s_ref[layer, rows, :] == 1)
            for i in range(Q):
                lam_ref[i, layer, rows, :] = out[i]
            sens_ref[layer, rows, :] = tile[Q] + design


def call(kernel, outs, scratch, *args, space=pltpu.VMEM):
    vmem = pl.BlockSpec(memory_space=pltpu.VMEM)
    return pl.pallas_call(
        kernel,
        out_shape=[jax.ShapeDtypeStruct(shape, jnp.float32) for shape in outs],
        in_specs=[pl.BlockSpec(memory_space=space)] * len(args),
        out_specs=[vmem] * len(outs),
        scratch_shapes=[pltpu.VMEM(shape, jnp.float32) if isinstance(shape, tuple) else shape for shape in scratch],
        compiler_params=pltpu.CompilerParams(vmem_limit_bytes=VMEM_LIMIT),
    )(*args)


def ring_pairs(planes, step):
    order = []
    for plane in range(planes):
        for block in range(GROUP):
            gray = (plane - block) % GROUP
            order.append((gray ^ (gray >> 1)) * planes + plane)
    return [(here, order[(at + step) % len(order)]) for at, here in enumerate(order)]


def fast_body(checkpoint, resistance, solid, adjoint_final):
    planes = lax.axis_size("gy")

    def trade(pieces):
        moved = list(pieces)
        for k in TRADES:
            moved[k] = lax.ppermute(pieces[k], "gx", [(i, i ^ k) for i in range(GROUP)])
        return moved

    def swap(value):
        return lax.ppermute(value, "gz", [(0, 1), (1, 0)])

    def ring(up, down):
        lo = lax.ppermute(up, ("gx", "gy"), ring_pairs(planes, 1))
        hi = lax.ppermute(down, ("gx", "gy"), ring_pairs(planes, -1))
        return lo, hi

    given = (checkpoint, resistance, solid, adjoint_final)
    pieces = call(
        send_kernel,
        [(FIELDS, 8, 128)] * GROUP,
        [(GROUP, FIELDS, 8, 128)]
        + [pltpu.VMEM(array.shape, array.dtype) for array in given]
        + [pltpu.SemaphoreType.DMA((len(given),))],
        *[pltpu.with_memory_space_constraint(array, pltpu.HBM) for array in given],
        space=pltpu.HBM,
    )
    fenced = lax.optimization_barrier((adjoint_final, *pieces))
    adjoint_pieces = call(
        send_adjoint_kernel,
        [(Q, 8, 128)] * GROUP,
        [(GROUP, Q, 8, 128), pltpu.VMEM(adjoint_final.shape, jnp.float32), pltpu.SemaphoreType.DMA],
        pltpu.with_memory_space_constraint(fenced[0], pltpu.HBM),
        space=pltpu.HBM,
    )
    pieces = trade(fenced[1:])
    own, up, down = call(
        turn_kernel,
        [(ROWS, ADJ, 8, 128), (len(FORWARD_UP), 8, 128), (len(FORWARD_DOWN), 8, 128)],
        [(FIELDS, 8 * ROWS, 128)],
        *pieces,
    )
    own_b = swap(own)
    (adj,) = call(turn_adjoint_kernel, [(ROWS, Q, 8, 128)], [(Q, 8 * ROWS, 128)], *trade(adjoint_pieces))
    adj_b = swap(adj)
    lo, hi = ring(up, down)
    lo_b, hi_b = swap(lo), swap(hi)
    lam, sens, mom1, mom2, rs, up, down = call(
        forward_kernel,
        [
            (ROWS, Q, 8, 256),
            (ROWS, 8, 128),
            (ROWS + 4, 4, 8, 256),
            (ROWS + 2, 4, 8, 256),
            (ROWS + 4, 2, 8, 256),
            (len(BACKWARD_UP) + strip_count(BACKWARD_UP, BACKWARD_REACH), 8, 128),
            (len(BACKWARD_DOWN) + strip_count(BACKWARD_DOWN, BACKWARD_REACH), 8, 128),
        ],
        [(ROWS + 6, Q, 8, 256), (ROWS + 4, Q, 8, 256), (ROWS + 2, Q, 8, 256), (ROWS + 2, Q, 8, 256)],
        *(own, own_b, adj, adj_b, lo, lo_b, hi, hi_b),
    )
    lo, hi = ring(up, down)
    l2_inner, sens = call(inner_backward_kernel, [(2, Q, 8, 256), (ROWS, 8, 128)], [], lam, sens, mom2, rs)
    pieces = call(
        backward_kernel,
        [(Q + 1, 8, 128)] * GROUP,
        [
            (ROWS + 6, Q, 8, 256),
            (ROWS + 4, Q, 8, 256),
            (ROWS + 2, Q, 8, 256),
            (ROWS + 4, 4, 8, 256),
            (Q + 1, 8 * ROWS, 128),
        ],
        *(lam, sens, mom1, mom2, rs, l2_inner, lo, hi),
    )
    pieces = trade(pieces)
    return tuple(
        call(
            finish_kernel,
            [checkpoint.shape, resistance.shape],
            [(GROUP, Q + 1, 8, 128)],
            checkpoint,
            resistance,
            solid,
            *pieces,
        )
    )


def padded_2(shard, sides, width):
    for axis, dim in sides:
        count, length = (lax.axis_size(axis), shard.shape[dim])
        up = [(i, (i + 1) % count) for i in range(count)]
        down = [(j, i) for i, j in up]
        last = lax.slice_in_dim(shard, length - width, length, axis=dim)
        leading = lax.slice_in_dim(shard, 0, width, axis=dim)
        before = lax.ppermute(last, axis, up)
        after = lax.ppermute(leading, axis, down)
        shard = jnp.concatenate([before, shard, after], axis=dim)
    return shard


def collide(populations, resistance, solid):
    lattice = jnp.array(VELOCITIES, jnp.float32)
    weights = jnp.array(WEIGHTS, jnp.float32).reshape(-1, 1, 1, 1)
    density = jnp.sum(populations, axis=0)
    momentum = jnp.tensordot(lattice, populations, axes=([0], [0]), precision=lax.Precision.HIGHEST)
    nothing = jnp.zeros_like(density)
    push = jnp.stack([BODY_FORCE * density, nothing, nothing]) - resistance[None] * momentum
    velocity = (momentum + RELAXATION * push) / density[None]
    projected = jnp.tensordot(lattice, velocity, axes=([1], [0]), precision=lax.Precision.HIGHEST)
    speed_squared = jnp.sum(velocity * velocity, axis=0)
    equilibrium = (
        weights
        * density[None]
        * (1.0 + 3.0 * projected + 4.5 * projected * projected - 1.5 * speed_squared[None])
    )
    relaxed = populations - (populations - equilibrium) / RELAXATION
    reflected = jnp.stack([populations[other] for other in OPPOSITE])
    return jnp.where(solid[None] == 1, reflected, relaxed)


def transport(field, sign):
    padded = padded_2(field, (("gx", 1), ("gy", 2), ("gz", 3)), 1)
    first, second, third = (field.shape[1], field.shape[2], field.shape[3])
    pieces = []
    for number, entry in enumerate(VELOCITIES):
        start_a = 1 - sign * entry[0]
        start_b = 1 - sign * entry[1]
        start_c = 1 - sign * entry[2]
        pieces.append(
            padded[
                number,
                start_a : start_a + first,
                start_b : start_b + second,
                start_c : start_c + third,
            ]
        )
    return jnp.stack(pieces)


def general_body(checkpoint, resistance, solid, adjoint_final):
    states = [checkpoint]
    current = checkpoint
    for step in range(STEPS - 1):
        current = transport(collide(current, resistance, solid), 1)
        states.append(current)
    adjoint = adjoint_final
    sensitivity = jnp.zeros_like(resistance)
    for step in reversed(range(STEPS)):
        pulled = transport(adjoint, -1)

        def local_collide(populations, design):
            return collide(populations, design, solid)

        result, backward = jax.vjp(local_collide, states[step], resistance)
        adjoint, design_part = backward(pulled)
        sensitivity = sensitivity + design_part
    return (adjoint, sensitivity)


def body(checkpoint, resistance, solid, adjoint_final):
    fits = (
        lax.axis_size("gx") == GROUP
        and lax.axis_size("gz") == 2
        and resistance.shape == (LAYERS, GROUP * ROWS, 128)
    )
    chosen = fast_body if fits else general_body
    return chosen(checkpoint, resistance, solid, adjoint_final)


def solution(mesh):
    in_specs = (
        P(None, "gx", "gy", "gz"),
        P("gx", "gy", "gz"),
        P("gx", "gy", "gz"),
        P(None, "gx", "gy", "gz"),
    )
    out_specs = (P(None, "gx", "gy", "gz"), P("gx", "gy", "gz"))
    return jax.shard_map(body, mesh=mesh, in_specs=in_specs, out_specs=out_specs, check_vma=False)
```

```python
import functools

import jax
import jax.numpy as jnp
from jax import lax
from jax.experimental import pallas as pl
from jax.experimental.pallas import tpu as pltpu
from jax.sharding import PartitionSpec as P

STEPS = 4


VELOCITIES = (
    (0, 0, 0),
    (1, 0, 0),
    (-1, 0, 0),
    (0, 1, 0),
    (0, -1, 0),
    (0, 0, 1),
    (0, 0, -1),
    (1, 1, 0),
    (-1, -1, 0),
    (1, -1, 0),
    (-1, 1, 0),
    (1, 0, 1),
    (-1, 0, -1),
    (1, 0, -1),
    (-1, 0, 1),
    (0, 1, 1),
    (0, -1, -1),
    (0, 1, -1),
    (0, -1, 1),
)
WEIGHTS = (1.0 / 3.0,) + (1.0 / 18.0,) * 6 + (1.0 / 36.0,) * 12
OPPOSITE = tuple((VELOCITIES.index((-entry[0], -entry[1], -entry[2])) for entry in VELOCITIES))
RELAXATION = 0.8
BODY_FORCE = 0.01

Q = len(VELOCITIES)
KEEP = 1.0 - 1.0 / RELAXATION
PUSH = RELAXATION * BODY_FORCE
VMEM_LIMIT = 16 * 1024 * 1024

GROUP = 4
ROWS = 4
LAYERS = 2
TRADES = (0, 3, 2, 1)
FORWARD_REACH, BACKWARD_REACH = 6, 3
RES, SOL, ADJ = Q, Q + 1, Q + 2
DOWNWARD = [i for i in range(Q) if VELOCITIES[i][1] > 0]
UPWARD = [i for i in range(Q) if VELOCITIES[i][1] < 0]
EDGES = -(-len(UPWARD) // 2)
FIELDS = ADJ + EDGES

FORWARD_UP = (
    [(3, i, -1) for i in range(Q)]
    + [(2, i, -2) for i in range(Q) if VELOCITIES[i][1] >= 0]
    + [(1, i, -3) for i in range(Q) if VELOCITIES[i][1] > 0]
    + [(3, RES, -1), (3, SOL, -1), (2, RES, -2), (2, SOL, -2)]
    + [(3, ADJ + i, -1) for i in range(Q) if VELOCITIES[i][1] < 0]
)
FORWARD_DOWN = (
    [(0, i, 4) for i in range(Q)]
    + [(1, i, 5) for i in range(Q) if VELOCITIES[i][1] <= 0]
    + [(2, i, 6) for i in range(Q) if VELOCITIES[i][1] < 0]
    + [(0, RES, 4), (0, SOL, 4), (1, RES, 5), (1, SOL, 5)]
    + [(0, ADJ + i, 4) for i in range(Q) if VELOCITIES[i][1] > 0]
)
OWN = [(row, field) for row in range(ROWS) for field in range(ADJ)]
OWN_ADJOINT = [(row, field) for row in range(ROWS) for field in range(Q)]
BACKWARD_UP = (
    [(3, i, -1) for i in range(Q)]
    + [(2, i, -2) for i in range(Q) if VELOCITIES[i][1] <= 0]
    + [(1, i, -3) for i in range(Q) if VELOCITIES[i][1] < 0]
    + [(2, Q + j, -2) for j in range(4)]
)
BACKWARD_DOWN = (
    [(0, i, 4) for i in range(Q)]
    + [(1, i, 5) for i in range(Q) if VELOCITIES[i][1] >= 0]
    + [(2, i, 6) for i in range(Q) if VELOCITIES[i][1] > 0]
    + [(1, Q + j, 5) for j in range(4)]
)


def moments(f):
    plus = [f[i] + f[i + 1] for i in range(1, Q, 2)]
    less = [f[i] - f[i + 1] for i in range(1, Q, 2)]
    density = f[0] + ((plus[0] + plus[1]) + (plus[2] + plus[3])) + ((plus[4] + plus[5]) + (plus[6] + (plus[7] + plus[8])))
    first = less[0] + ((less[3] + less[4]) + (less[5] + less[6]))
    second = less[1] + ((less[3] - less[4]) + (less[7] + less[8]))
    third = less[2] + ((less[5] - less[6]) + (less[7] - less[8]))
    inverse = 1.0 / density
    return density, first * inverse, second * inverse, third * inverse


def slots_of(reach):
    return 128 // (2 * reach)


def strip_count(table, reach):
    return -(-len(table) // slots_of(reach))


def pack_strips(tiles, reach):
    lane = lax.broadcasted_iota(jnp.int32, (8, 128), 1)
    packed = []
    for number, tile in enumerate(tiles):
        start = 2 * reach * (number % slots_of(reach))
        moved = pltpu.roll(tile, start + reach, axis=1)
        if start == 0:
            packed.append(moved)
        else:
            packed[-1] = jnp.where(lane >= start, moved, packed[-1])
    return packed


def unpack_strip(packed, number, reach):
    start = 2 * reach * (number % slots_of(reach))
    return pltpu.roll(packed[number // slots_of(reach)], 128 - start - reach, axis=1)


def along(i, x, y, z):
    total = None
    for sign, part in zip(VELOCITIES[i], (x, y, z)):
        if sign == 0:
            continue
        if total is None:
            total = part if sign > 0 else -part
        else:
            total = total + part if sign > 0 else total - part
    return total


def inward(row, last, sign):
    if row == 0:
        return [i for i in range(Q) if sign * VELOCITIES[i][1] > 0]
    if row == last:
        return [i for i in range(Q) if sign * VELOCITIES[i][1] < 0]
    return list(range(Q))


def collide_lists(f, density, vx, vy, vz, resistance, solid):
    damp = 1.0 - RELAXATION * resistance
    ux, uy, uz = damp * vx + PUSH, damp * vy, damp * vz
    base = 1.0 - 1.5 * (ux * ux + uy * uy + uz * uz)
    scaled = {w: density * (w / RELAXATION) for w in sorted(set(WEIGHTS))}
    out = [jnp.where(solid, f[0], KEEP * f[0] + scaled[WEIGHTS[0]] * base)]
    for i in range(1, Q, 2):
        projected = along(i, ux, uy, uz)
        weight = scaled[WEIGHTS[i]]
        even = weight * (base + 4.5 * (projected * projected))
        odd = weight * (3.0 * projected)
        out.append(jnp.where(solid, f[i + 1], KEEP * f[i] + (even + odd)))
        out.append(jnp.where(solid, f[i], KEEP * f[i + 1] + (even - odd)))
    return out


def adjoint_lists(mu, density, vx, vy, vz, resistance, solid):
    damp = 1.0 - RELAXATION * resistance
    ux, uy, uz = damp * vx + PUSH, damp * vy, damp * vz
    plus = [mu[i] + mu[i + 1] for i in range(1, Q, 2)]
    less = [mu[i] - mu[i + 1] for i in range(1, Q, 2)]
    rest, axis, diagonal = (w / RELAXATION for w in (WEIGHTS[0], WEIGHTS[1], WEIGHTS[7]))
    xy, xz, yz = plus[3] + plus[4], plus[5] + plus[6], plus[7] + plus[8]
    zeroth = rest * mu[0] + axis * ((plus[0] + plus[1]) + plus[2]) + diagonal * ((xy + xz) + yz)
    nx = axis * less[0] + diagonal * ((less[3] + less[4]) + (less[5] + less[6]))
    ny = axis * less[1] + diagonal * ((less[3] - less[4]) + (less[7] + less[8]))
    nz = axis * less[2] + diagonal * ((less[5] - less[6]) + (less[7] - less[8]))
    nxx = axis * plus[0] + diagonal * (xy + xz)
    nyy = axis * plus[1] + diagonal * (xy + yz)
    nzz = axis * plus[2] + diagonal * (xz + yz)
    nxy = diagonal * (plus[3] - plus[4])
    nxz = diagonal * (plus[5] - plus[6])
    nyz = diagonal * (plus[7] - plus[8])
    tx = nxx * ux + nxy * uy + nxz * uz
    ty = nxy * ux + nyy * uy + nyz * uz
    tz = nxz * ux + nyz * uy + nzz * uz
    hx = 3.0 * (nx - ux * zeroth) + 9.0 * tx
    hy = 3.0 * (ny - uy * zeroth) + 9.0 * ty
    hz = 3.0 * (nz - uz * zeroth) + 9.0 * tz
    pulled = vx * hx + vy * hy + vz * hz
    square = ux * ux + uy * uy + uz * uz
    scalar = (
        zeroth * (1.0 - 1.5 * square)
        + 3.0 * (nx * ux + ny * uy + nz * uz)
        + 4.5 * (tx * ux + ty * uy + tz * uz)
        - damp * pulled
    )
    qx, qy, qz = damp * hx, damp * hy, damp * hz
    out = [jnp.where(solid, mu[0], KEEP * mu[0] + scalar)]
    for i in range(1, Q, 2):
        slope = along(i, qx, qy, qz)
        out.append(jnp.where(solid, mu[i + 1], KEEP * mu[i] + (scalar + slope)))
        out.append(jnp.where(solid, mu[i], KEEP * mu[i + 1] + (scalar - slope)))
    design = jnp.where(solid, 0.0, (-RELAXATION) * density * pulled)
    return out, design


def shifted(value, i, sign):
    first, _, third = VELOCITIES[i]
    if first:
        value = pltpu.roll(value, (sign * first) % value.shape[0], axis=0)
    if third:
        value = pltpu.roll(value, (sign * third) % value.shape[1], axis=1)
    return value


def block_of(number):
    return (lax.axis_index("gy") + GROUP - (number ^ (number >> 1))) % GROUP


def send_kernel(*refs):
    given, outs, blocks, held, sems = refs[:4], refs[4 : 4 + GROUP], refs[4 + GROUP], refs[5 + GROUP : 9 + GROUP], refs[-1]
    copies = [pltpu.make_async_copy(source, target, sems.at[at]) for at, (source, target) in enumerate(zip(given, held))]
    for copy in copies:
        copy.start()
    for copy in copies[:3]:
        copy.wait()
    f_ref, r_ref, s_ref, a_ref = held
    for half in range(2):
        rows = pl.ds(8 * half, 8)
        tiles = []
        for layer in range(LAYERS):
            f = [f_ref[i, layer, rows, :] for i in range(Q)]
            resistance, kind = r_ref[layer, rows, :], s_ref[layer, rows, :]
            out = collide_lists(f, *moments(f), resistance, kind == 1)
            tiles.append(out + [resistance, kind.astype(jnp.float32)])
        for field in range(ADJ):
            first, second = tiles[0][field], tiles[1][field]
            blocks[2 * half, field] = jnp.concatenate([first[:4], second[:4]], axis=0)
            blocks[2 * half + 1, field] = jnp.concatenate([first[4:], second[4:]], axis=0)
    copies[3].wait()
    for block in range(GROUP):
        for edge in range(EDGES):
            rows = []
            for layer in range(LAYERS):
                for group, row in ((DOWNWARD, 0), (UPWARD, ROWS - 1)):
                    for number in (2 * edge, 2 * edge + 1):
                        i = group[min(number, len(group) - 1)]
                        rows.append(a_ref[i, layer, pl.ds(ROWS * block + row, 1), :])
            blocks[block, ADJ + edge] = jnp.concatenate(rows, axis=0)
    here = lax.axis_index("gx")
    for k, out in zip(TRADES, outs):
        out[...] = blocks[block_of(here ^ k)]


def send_adjoint_kernel(a_hbm, *refs):
    outs, (blocks, a_ref, sem) = refs[:GROUP], refs[GROUP:]
    copy = pltpu.make_async_copy(a_hbm, a_ref, sem)
    copy.start()
    copy.wait()
    for block in range(GROUP):
        for i in range(Q):
            blocks[block, i] = jnp.concatenate([a_ref[i, layer, pl.ds(4 * block, 4), :] for layer in range(LAYERS)], axis=0)
    here = lax.axis_index("gx")
    for k, out in zip(TRADES, outs):
        out[...] = blocks[block_of(here ^ k)]


def gather_pieces(ins, flat):
    here = lax.axis_index("gx")
    for k, piece in zip(TRADES, ins):
        start = 8 * (here ^ k)
        for field in range(flat.shape[0]):
            flat[field, pl.ds(pl.multiple_of(start, 8), 8), :] = piece[field]


def turn_kernel(*refs):
    ins, (own, up, down, flat) = refs[:GROUP], refs[GROUP:]
    gather_pieces(ins, flat)
    for field in range(ADJ):
        for row in range(ROWS):
            own[row, field] = flat[field, pl.ds(row, 8, stride=ROWS), :]
    for table, part in ((FORWARD_UP, up), (FORWARD_DOWN, down)):
        for number, (row, field, _) in enumerate(table):
            if field < ADJ:
                part[number] = own[row, field]
            else:
                group, base = (UPWARD, 2) if row else (DOWNWARD, 0)
                edge, slot = divmod(group.index(field - ADJ), 2)
                part[number] = flat[ADJ + edge, pl.ds(base + slot, 8, stride=ROWS), :]


def turn_adjoint_kernel(*refs):
    ins, (adj, flat) = refs[:GROUP], refs[GROUP:]
    gather_pieces(ins, flat)
    for field in range(Q):
        for row in range(ROWS):
            adj[row, field] = flat[field, pl.ds(row, 8, stride=ROWS), :]


def stream_pull(source, row, sign):
    return [shifted(source[row + 1 - sign * VELOCITIES[i][1], i], i, sign) for i in range(Q)]


def place(target, own_half, packed, number, reach):
    target[:, :128] = own_half
    target[:, 128:] = unpack_strip(packed, number, reach)


def forward_kernel(
    own_a, own_b, adj_a, adj_b, lo_a, lo_b, hi_a, hi_b, lam_ref, sens_ref, mom1, mom2, rs_ref, up, down, p0, p1, p2, a4
):
    def target(field, row):
        if field < Q:
            return p0.at[row + 3, field]
        return rs_ref.at[row + 2, field - RES] if field < ADJ else a4.at[row + 1, field - ADJ]

    for side, own, adj in ((0, own_a, adj_a), (1, own_b, adj_b)):
        lanes = slice(128 * side, 128 * side + 128)
        for row, field in OWN:
            target(field, row)[:, lanes] = own[row, field]
        for row, field in OWN_ADJOINT:
            target(ADJ + field, row)[:, lanes] = adj[row, field]
    for table, parts in ((FORWARD_UP, (lo_a, lo_b)), (FORWARD_DOWN, (hi_a, hi_b))):
        for side, part in enumerate(parts):
            for number, (_, field, row) in enumerate(table):
                target(field, row)[:, slice(128 * side, 128 * side + 128)] = part[number]
    for row in range(ROWS + 4):
        f = stream_pull(p0, row, 1)
        moment = moments(f)
        for j in range(4):
            mom1[row, j] = moment[j]
        out = collide_lists(f, *moment, rs_ref[row, 0], rs_ref[row, 1] == 1.0)
        for i in inward(row, ROWS + 3, 1):
            p1[row, i] = out[i]
    for row in range(ROWS + 2):
        f = stream_pull(p1, row, 1)
        moment = moments(f)
        for j in range(4):
            mom2[row, j] = moment[j]
        out = collide_lists(f, *moment, rs_ref[row + 1, 0], rs_ref[row + 1, 1] == 1.0)
        for i in inward(row, ROWS + 1, 1):
            p2[row, i] = out[i]
    for row in range(ROWS):
        moment = moments(stream_pull(p2, row, 1))
        mu = stream_pull(a4, row, -1)
        out, design = adjoint_lists(mu, *moment, rs_ref[row + 2, 0], rs_ref[row + 2, 1] == 1.0)
        for i in range(Q):
            lam_ref[row, i] = out[i]
        sens_ref[row] = design[:, :128]
    for table, part in ((BACKWARD_UP, up), (BACKWARD_DOWN, down)):
        others = []
        for number, (row, field, _) in enumerate(table):
            source = lam_ref[row, field] if field < Q else mom2[row + 1, field - Q]
            part[number] = source[:, :128]
            others.append(source[:, 128:])
        for number, tile in enumerate(pack_strips(others, BACKWARD_REACH)):
            part[len(table) + number] = tile


def inner_backward_kernel(lam_ref, sens_ref, mom2, rs_ref, l2, sens_out):
    for row in (0, ROWS - 1):
        sens_out[row] = sens_ref[row]
    for row in range(ROWS - 2):
        mu = stream_pull(lam_ref, row, -1)
        moment = [mom2[row + 2, j] for j in range(4)]
        out, design = adjoint_lists(mu, *moment, rs_ref[row + 3, 0], rs_ref[row + 3, 1] == 1.0)
        for i in range(Q):
            l2[row, i] = out[i]
        sens_out[row + 1] = sens_ref[row + 1] + design[:, :128]


def backward_kernel(lam_ref, sens_ref, mom1, mom2, rs_ref, l2_inner, lo, hi, *refs):
    outs, (l3, l2, l1, m2, flat) = refs[:GROUP], refs[GROUP:]
    for row in range(ROWS):
        for i in range(Q):
            l3[row + 3, i] = lam_ref[row, i]
    for row in range(ROWS + 2):
        for j in range(4):
            m2[row + 1, j] = mom2[row, j]
    for table, part in ((BACKWARD_UP, lo), (BACKWARD_DOWN, hi)):
        packed = [part[len(table) + number] for number in range(strip_count(table, BACKWARD_REACH))]
        for number, (_, field, row) in enumerate(table):
            target = l3.at[row + 3, field] if field < Q else m2.at[row + 2, field - Q]
            place(target, part[number], packed, number, BACKWARD_REACH)
    designs = [sens_ref[row] for row in range(ROWS)]
    for row in range(ROWS + 4):
        if 3 <= row < ROWS + 1:
            for i in range(Q):
                l2[row, i] = l2_inner[row - 3, i]
            continue
        mu = stream_pull(l3, row, -1)
        out, design = adjoint_lists(mu, *[m2[row, j] for j in range(4)], rs_ref[row, 0], rs_ref[row, 1] == 1.0)
        for i in inward(row, ROWS + 3, -1):
            l2[row, i] = out[i]
        if 2 <= row < ROWS + 2:
            designs[row - 2] = designs[row - 2] + design[:, :128]
    for row in range(ROWS + 2):
        mu = stream_pull(l2, row, -1)
        moment = [mom1[row + 1, j] for j in range(4)]
        out, design = adjoint_lists(mu, *moment, rs_ref[row + 1, 0], rs_ref[row + 1, 1] == 1.0)
        for i in inward(row, ROWS + 1, -1):
            l1[row, i] = out[i]
        if 1 <= row < ROWS + 1:
            designs[row - 1] = designs[row - 1] + design[:, :128]
    for row in range(ROWS):
        flat[Q, pl.ds(row, 8, stride=ROWS), :] = designs[row]
        mu = stream_pull(l1, row, -1)
        for i in range(Q):
            flat[i, pl.ds(row, 8, stride=ROWS), :] = mu[i][:, :128]
    here = lax.axis_index("gx")
    for k, out in zip(TRADES, outs):
        start = 8 * (here ^ k)
        for i in range(Q + 1):
            out[i] = flat[i, pl.ds(pl.multiple_of(start, 8), 8), :]


def finish_kernel(f_ref, r_ref, s_ref, *refs):
    ins, (lam_ref, sens_ref, blocks) = refs[:GROUP], refs[GROUP:]
    here = lax.axis_index("gx")
    for k, piece in zip(TRADES, ins):
        blocks[block_of(here ^ k)] = piece[...]
    for half in range(2):
        rows = pl.ds(8 * half, 8)
        for layer in range(LAYERS):
            part = slice(4 * layer, 4 * layer + 4)
            tile = [
                jnp.concatenate([blocks[2 * half, i, part, :], blocks[2 * half + 1, i, part, :]], axis=0)
                for i in range(Q + 1)
            ]
            f = [f_ref[i, layer, rows, :] for i in range(Q)]
            out, design = adjoint_lists(tile[:Q], *moments(f), r_ref[layer, rows, :], s_ref[layer, rows, :] == 1)
            for i in range(Q):
                lam_ref[i, layer, rows, :] = out[i]
            sens_ref[layer, rows, :] = tile[Q] + design


def call(kernel, outs, scratch, *args, space=pltpu.VMEM):
    vmem = pl.BlockSpec(memory_space=pltpu.VMEM)
    return pl.pallas_call(
        kernel,
        out_shape=[jax.ShapeDtypeStruct(shape, jnp.float32) for shape in outs],
        in_specs=[pl.BlockSpec(memory_space=space)] * len(args),
        out_specs=[vmem] * len(outs),
        scratch_shapes=[pltpu.VMEM(shape, jnp.float32) if isinstance(shape, tuple) else shape for shape in scratch],
        compiler_params=pltpu.CompilerParams(vmem_limit_bytes=VMEM_LIMIT),
    )(*args)


def ring_pairs(planes, step):
    order = []
    for plane in range(planes):
        for block in range(GROUP):
            gray = (plane - block) % GROUP
            order.append((gray ^ (gray >> 1)) * planes + plane)
    return [(here, order[(at + step) % len(order)]) for at, here in enumerate(order)]


def fast_body(checkpoint, resistance, solid, adjoint_final):
    planes = lax.axis_size("gy")

    def trade(pieces):
        moved = [pieces[0]]
        for number, k in enumerate(TRADES[1:], 1):
            moved.append(lax.ppermute(pieces[number], "gx", [(i, i ^ k) for i in range(GROUP)]))
        return moved

    def swap(value):
        return lax.ppermute(value, "gz", [(0, 1), (1, 0)])

    def ring(up, down):
        lo = lax.ppermute(up, ("gx", "gy"), ring_pairs(planes, 1))
        hi = lax.ppermute(down, ("gx", "gy"), ring_pairs(planes, -1))
        return lo, hi

    given = (checkpoint, resistance, solid, adjoint_final)
    pieces = call(
        send_kernel,
        [(FIELDS, 8, 128)] * GROUP,
        [(GROUP, FIELDS, 8, 128)]
        + [pltpu.VMEM(array.shape, array.dtype) for array in given]
        + [pltpu.SemaphoreType.DMA((len(given),))],
        *[pltpu.with_memory_space_constraint(array, pltpu.HBM) for array in given],
        space=pltpu.HBM,
    )
    fenced = lax.optimization_barrier((adjoint_final, *pieces))
    adjoint_pieces = call(
        send_adjoint_kernel,
        [(Q, 8, 128)] * GROUP,
        [(GROUP, Q, 8, 128), pltpu.VMEM(adjoint_final.shape, jnp.float32), pltpu.SemaphoreType.DMA],
        pltpu.with_memory_space_constraint(fenced[0], pltpu.HBM),
        space=pltpu.HBM,
    )
    pieces = trade(fenced[1:])
    own, up, down = call(
        turn_kernel,
        [(ROWS, ADJ, 8, 128), (len(FORWARD_UP), 8, 128), (len(FORWARD_DOWN), 8, 128)],
        [(FIELDS, 8 * ROWS, 128)],
        *pieces,
    )
    own_b = swap(own)
    (adj,) = call(turn_adjoint_kernel, [(ROWS, Q, 8, 128)], [(Q, 8 * ROWS, 128)], *trade(adjoint_pieces))
    adj_b = swap(adj)
    lo, hi = ring(up, down)
    lo_b, hi_b = swap(lo), swap(hi)
    lam, sens, mom1, mom2, rs, up, down = call(
        forward_kernel,
        [
            (ROWS, Q, 8, 256),
            (ROWS, 8, 128),
            (ROWS + 4, 4, 8, 256),
            (ROWS + 2, 4, 8, 256),
            (ROWS + 4, 2, 8, 256),
            (len(BACKWARD_UP) + strip_count(BACKWARD_UP, BACKWARD_REACH), 8, 128),
            (len(BACKWARD_DOWN) + strip_count(BACKWARD_DOWN, BACKWARD_REACH), 8, 128),
        ],
        [(ROWS + 6, Q, 8, 256), (ROWS + 4, Q, 8, 256), (ROWS + 2, Q, 8, 256), (ROWS + 2, Q, 8, 256)],
        *(own, own_b, adj, adj_b, lo, lo_b, hi, hi_b),
    )
    lo, hi = ring(up, down)
    l2_inner, sens = call(inner_backward_kernel, [(2, Q, 8, 256), (ROWS, 8, 128)], [], lam, sens, mom2, rs)
    pieces = call(
        backward_kernel,
        [(Q + 1, 8, 128)] * GROUP,
        [
            (ROWS + 6, Q, 8, 256),
            (ROWS + 4, Q, 8, 256),
            (ROWS + 2, Q, 8, 256),
            (ROWS + 4, 4, 8, 256),
            (Q + 1, 8 * ROWS, 128),
        ],
        *(lam, sens, mom1, mom2, rs, l2_inner, lo, hi),
    )
    pieces = trade(pieces)
    return tuple(
        call(
            finish_kernel,
            [checkpoint.shape, resistance.shape],
            [(GROUP, Q + 1, 8, 128)],
            checkpoint,
            resistance,
            solid,
            *pieces,
        )
    )


def padded_2(shard, sides, width):
    for axis, dim in sides:
        count, length = (lax.axis_size(axis), shard.shape[dim])
        up = [(i, (i + 1) % count) for i in range(count)]
        down = [(j, i) for i, j in up]
        last = lax.slice_in_dim(shard, length - width, length, axis=dim)
        leading = lax.slice_in_dim(shard, 0, width, axis=dim)
        before = lax.ppermute(last, axis, up)
        after = lax.ppermute(leading, axis, down)
        shard = jnp.concatenate([before, shard, after], axis=dim)
    return shard


def collide(populations, resistance, solid):
    lattice = jnp.array(VELOCITIES, jnp.float32)
    weights = jnp.array(WEIGHTS, jnp.float32).reshape(-1, 1, 1, 1)
    density = jnp.sum(populations, axis=0)
    momentum = jnp.tensordot(lattice, populations, axes=([0], [0]), precision=lax.Precision.HIGHEST)
    nothing = jnp.zeros_like(density)
    push = jnp.stack([BODY_FORCE * density, nothing, nothing]) - resistance[None] * momentum
    velocity = (momentum + RELAXATION * push) / density[None]
    projected = jnp.tensordot(lattice, velocity, axes=([1], [0]), precision=lax.Precision.HIGHEST)
    speed_squared = jnp.sum(velocity * velocity, axis=0)
    equilibrium = (
        weights
        * density[None]
        * (1.0 + 3.0 * projected + 4.5 * projected * projected - 1.5 * speed_squared[None])
    )
    relaxed = populations - (populations - equilibrium) / RELAXATION
    reflected = jnp.stack([populations[other] for other in OPPOSITE])
    return jnp.where(solid[None] == 1, reflected, relaxed)


def transport(field, sign):
    padded = padded_2(field, (("gx", 1), ("gy", 2), ("gz", 3)), 1)
    first, second, third = (field.shape[1], field.shape[2], field.shape[3])
    pieces = []
    for number, entry in enumerate(VELOCITIES):
        start_a = 1 - sign * entry[0]
        start_b = 1 - sign * entry[1]
        start_c = 1 - sign * entry[2]
        pieces.append(
            padded[
                number,
                start_a : start_a + first,
                start_b : start_b + second,
                start_c : start_c + third,
            ]
        )
    return jnp.stack(pieces)


def general_body(checkpoint, resistance, solid, adjoint_final):
    states = [checkpoint]
    current = checkpoint
    for step in range(STEPS - 1):
        current = transport(collide(current, resistance, solid), 1)
        states.append(current)
    adjoint = adjoint_final
    sensitivity = jnp.zeros_like(resistance)
    for step in reversed(range(STEPS)):
        pulled = transport(adjoint, -1)

        def local_collide(populations, design):
            return collide(populations, design, solid)

        result, backward = jax.vjp(local_collide, states[step], resistance)
        adjoint, design_part = backward(pulled)
        sensitivity = sensitivity + design_part
    return (adjoint, sensitivity)


def body(checkpoint, resistance, solid, adjoint_final):
    fits = (
        lax.axis_size("gx") == GROUP
        and lax.axis_size("gz") == 2
        and resistance.shape == (LAYERS, GROUP * ROWS, 128)
    )
    chosen = fast_body if fits else general_body
    return chosen(checkpoint, resistance, solid, adjoint_final)


def solution(mesh):
    in_specs = (
        P(None, "gx", "gy", "gz"),
        P("gx", "gy", "gz"),
        P("gx", "gy", "gz"),
        P(None, "gx", "gy", "gz"),
    )
    out_specs = (P(None, "gx", "gy", "gz"), P("gx", "gy", "gz"))
    return jax.shard_map(body, mesh=mesh, in_specs=in_specs, out_specs=out_specs, check_vma=False)
```

```python
import functools

import jax
import jax.numpy as jnp
from jax import lax
from jax.experimental import pallas as pl
from jax.experimental.pallas import tpu as pltpu
from jax.sharding import PartitionSpec as P

STEPS = 4


VELOCITIES = (
    (0, 0, 0),
    (1, 0, 0),
    (-1, 0, 0),
    (0, 1, 0),
    (0, -1, 0),
    (0, 0, 1),
    (0, 0, -1),
    (1, 1, 0),
    (-1, -1, 0),
    (1, -1, 0),
    (-1, 1, 0),
    (1, 0, 1),
    (-1, 0, -1),
    (1, 0, -1),
    (-1, 0, 1),
    (0, 1, 1),
    (0, -1, -1),
    (0, 1, -1),
    (0, -1, 1),
)
WEIGHTS = (1.0 / 3.0,) + (1.0 / 18.0,) * 6 + (1.0 / 36.0,) * 12
OPPOSITE = tuple((VELOCITIES.index((-entry[0], -entry[1], -entry[2])) for entry in VELOCITIES))
RELAXATION = 0.8
BODY_FORCE = 0.01

Q = len(VELOCITIES)
KEEP = 1.0 - 1.0 / RELAXATION
PUSH = RELAXATION * BODY_FORCE
VMEM_LIMIT = 16 * 1024 * 1024

GROUP = 4
ROWS = 4
LAYERS = 2
TRADES = (0, 3, 2, 1)
FORWARD_REACH, BACKWARD_REACH = 6, 3
RES, SOL, ADJ = Q, Q + 1, Q + 2
DOWNWARD = [i for i in range(Q) if VELOCITIES[i][1] > 0]
UPWARD = [i for i in range(Q) if VELOCITIES[i][1] < 0]
EDGES = -(-len(UPWARD) // 2)
FIELDS = ADJ + EDGES

FORWARD_UP = (
    [(3, i, -1) for i in range(Q)]
    + [(2, i, -2) for i in range(Q) if VELOCITIES[i][1] >= 0]
    + [(1, i, -3) for i in range(Q) if VELOCITIES[i][1] > 0]
    + [(3, RES, -1), (3, SOL, -1), (2, RES, -2), (2, SOL, -2)]
    + [(3, ADJ + i, -1) for i in range(Q) if VELOCITIES[i][1] < 0]
)
FORWARD_DOWN = (
    [(0, i, 4) for i in range(Q)]
    + [(1, i, 5) for i in range(Q) if VELOCITIES[i][1] <= 0]
    + [(2, i, 6) for i in range(Q) if VELOCITIES[i][1] < 0]
    + [(0, RES, 4), (0, SOL, 4), (1, RES, 5), (1, SOL, 5)]
    + [(0, ADJ + i, 4) for i in range(Q) if VELOCITIES[i][1] > 0]
)
OWN = [(row, field) for row in range(ROWS) for field in range(ADJ)]
OWN_ADJOINT = [(row, field) for row in range(ROWS) for field in range(Q)]
BACKWARD_UP = (
    [(3, i, -1) for i in range(Q)]
    + [(2, i, -2) for i in range(Q) if VELOCITIES[i][1] <= 0]
    + [(1, i, -3) for i in range(Q) if VELOCITIES[i][1] < 0]
    + [(2, Q + j, -2) for j in range(1, 4)]
)
BACKWARD_DOWN = (
    [(0, i, 4) for i in range(Q)]
    + [(1, i, 5) for i in range(Q) if VELOCITIES[i][1] >= 0]
    + [(2, i, 6) for i in range(Q) if VELOCITIES[i][1] > 0]
    + [(1, Q + j, 5) for j in range(1, 4)]
)


def moments(f):
    plus = [f[i] + f[i + 1] for i in range(1, Q, 2)]
    less = [f[i] - f[i + 1] for i in range(1, Q, 2)]
    density = f[0] + ((plus[0] + plus[1]) + (plus[2] + plus[3])) + ((plus[4] + plus[5]) + (plus[6] + (plus[7] + plus[8])))
    first = less[0] + ((less[3] + less[4]) + (less[5] + less[6]))
    second = less[1] + ((less[3] - less[4]) + (less[7] + less[8]))
    third = less[2] + ((less[5] - less[6]) + (less[7] - less[8]))
    inverse = 1.0 / density
    return density, first * inverse, second * inverse, third * inverse


def slots_of(reach):
    return 128 // (2 * reach)


def strip_count(table, reach):
    return -(-len(table) // slots_of(reach))


def pack_strips(tiles, reach):
    lane = lax.broadcasted_iota(jnp.int32, (8, 128), 1)
    packed = []
    for number, tile in enumerate(tiles):
        start = 2 * reach * (number % slots_of(reach))
        moved = pltpu.roll(tile, start + reach, axis=1)
        if start == 0:
            packed.append(moved)
        else:
            packed[-1] = jnp.where(lane >= start, moved, packed[-1])
    return packed


def unpack_strip(packed, number, reach):
    start = 2 * reach * (number % slots_of(reach))
    return pltpu.roll(packed[number // slots_of(reach)], 128 - start - reach, axis=1)


def along(i, x, y, z):
    total = None
    for sign, part in zip(VELOCITIES[i], (x, y, z)):
        if sign == 0:
            continue
        if total is None:
            total = part if sign > 0 else -part
        else:
            total = total + part if sign > 0 else total - part
    return total


def inward(row, last, sign):
    if row == 0:
        return [i for i in range(Q) if sign * VELOCITIES[i][1] > 0]
    if row == last:
        return [i for i in range(Q) if sign * VELOCITIES[i][1] < 0]
    return list(range(Q))


def collide_lists(f, density, vx, vy, vz, resistance, solid):
    damp = 1.0 - RELAXATION * resistance
    ux, uy, uz = damp * vx + PUSH, damp * vy, damp * vz
    base = 1.0 - 1.5 * (ux * ux + uy * uy + uz * uz)
    scaled = {w: density * (w / RELAXATION) for w in sorted(set(WEIGHTS))}
    out = [jnp.where(solid, f[0], KEEP * f[0] + scaled[WEIGHTS[0]] * base)]
    for i in range(1, Q, 2):
        projected = along(i, ux, uy, uz)
        weight = scaled[WEIGHTS[i]]
        even = weight * (base + 4.5 * (projected * projected))
        odd = weight * (3.0 * projected)
        out.append(jnp.where(solid, f[i + 1], KEEP * f[i] + (even + odd)))
        out.append(jnp.where(solid, f[i], KEEP * f[i + 1] + (even - odd)))
    return out


def adjoint_lists(mu, density, vx, vy, vz, resistance, solid):
    damp = 1.0 - RELAXATION * resistance
    ux, uy, uz = damp * vx + PUSH, damp * vy, damp * vz
    plus = [mu[i] + mu[i + 1] for i in range(1, Q, 2)]
    less = [mu[i] - mu[i + 1] for i in range(1, Q, 2)]
    rest, axis, diagonal = (w / RELAXATION for w in (WEIGHTS[0], WEIGHTS[1], WEIGHTS[7]))
    xy, xz, yz = plus[3] + plus[4], plus[5] + plus[6], plus[7] + plus[8]
    zeroth = rest * mu[0] + axis * ((plus[0] + plus[1]) + plus[2]) + diagonal * ((xy + xz) + yz)
    nx = axis * less[0] + diagonal * ((less[3] + less[4]) + (less[5] + less[6]))
    ny = axis * less[1] + diagonal * ((less[3] - less[4]) + (less[7] + less[8]))
    nz = axis * less[2] + diagonal * ((less[5] - less[6]) + (less[7] - less[8]))
    nxx = axis * plus[0] + diagonal * (xy + xz)
    nyy = axis * plus[1] + diagonal * (xy + yz)
    nzz = axis * plus[2] + diagonal * (xz + yz)
    nxy = diagonal * (plus[3] - plus[4])
    nxz = diagonal * (plus[5] - plus[6])
    nyz = diagonal * (plus[7] - plus[8])
    tx = nxx * ux + nxy * uy + nxz * uz
    ty = nxy * ux + nyy * uy + nyz * uz
    tz = nxz * ux + nyz * uy + nzz * uz
    hx = 3.0 * (nx - ux * zeroth) + 9.0 * tx
    hy = 3.0 * (ny - uy * zeroth) + 9.0 * ty
    hz = 3.0 * (nz - uz * zeroth) + 9.0 * tz
    pulled = vx * hx + vy * hy + vz * hz
    square = ux * ux + uy * uy + uz * uz
    scalar = (
        zeroth * (1.0 - 1.5 * square)
        + 3.0 * (nx * ux + ny * uy + nz * uz)
        + 4.5 * (tx * ux + ty * uy + tz * uz)
        - damp * pulled
    )
    qx, qy, qz = damp * hx, damp * hy, damp * hz
    out = [jnp.where(solid, mu[0], KEEP * mu[0] + scalar)]
    for i in range(1, Q, 2):
        slope = along(i, qx, qy, qz)
        out.append(jnp.where(solid, mu[i + 1], KEEP * mu[i] + (scalar + slope)))
        out.append(jnp.where(solid, mu[i], KEEP * mu[i + 1] + (scalar - slope)))
    design = jnp.where(solid, 0.0, (-RELAXATION) * density * pulled)
    return out, design


def shifted(value, i, sign):
    first, _, third = VELOCITIES[i]
    if first:
        value = pltpu.roll(value, (sign * first) % value.shape[0], axis=0)
    if third:
        value = pltpu.roll(value, (sign * third) % value.shape[1], axis=1)
    return value


def block_of(number):
    return (lax.axis_index("gy") + GROUP - (number ^ (number >> 1))) % GROUP


def send_kernel(*refs):
    given, outs, blocks, held, sems = refs[:4], refs[4 : 4 + GROUP], refs[4 + GROUP], refs[5 + GROUP : 9 + GROUP], refs[-1]
    copies = [pltpu.make_async_copy(source, target, sems.at[at]) for at, (source, target) in enumerate(zip(given, held))]
    for copy in copies:
        copy.start()
    for copy in copies[:3]:
        copy.wait()
    f_ref, r_ref, s_ref, a_ref = held
    for half in range(2):
        rows = pl.ds(8 * half, 8)
        tiles = []
        for layer in range(LAYERS):
            f = [f_ref[i, layer, rows, :] for i in range(Q)]
            resistance, kind = r_ref[layer, rows, :], s_ref[layer, rows, :]
            out = collide_lists(f, *moments(f), resistance, kind == 1)
            tiles.append(out + [resistance, kind.astype(jnp.float32)])
        for field in range(ADJ):
            first, second = tiles[0][field], tiles[1][field]
            blocks[2 * half, field] = jnp.concatenate([first[:4], second[:4]], axis=0)
            blocks[2 * half + 1, field] = jnp.concatenate([first[4:], second[4:]], axis=0)
    copies[3].wait()
    for block in range(GROUP):
        for edge in range(EDGES):
            rows = []
            for layer in range(LAYERS):
                for group, row in ((DOWNWARD, 0), (UPWARD, ROWS - 1)):
                    for number in (2 * edge, 2 * edge + 1):
                        i = group[min(number, len(group) - 1)]
                        rows.append(a_ref[i, layer, pl.ds(ROWS * block + row, 1), :])
            blocks[block, ADJ + edge] = jnp.concatenate(rows, axis=0)
    here = lax.axis_index("gx")
    for k, out in zip(TRADES, outs):
        out[...] = blocks[block_of(here ^ k)]


def send_adjoint_kernel(a_hbm, *refs):
    outs, (blocks, a_ref, sem) = refs[:GROUP], refs[GROUP:]
    copy = pltpu.make_async_copy(a_hbm, a_ref, sem)
    copy.start()
    copy.wait()
    for block in range(GROUP):
        for i in range(Q):
            blocks[block, i] = jnp.concatenate([a_ref[i, layer, pl.ds(4 * block, 4), :] for layer in range(LAYERS)], axis=0)
    here = lax.axis_index("gx")
    for k, out in zip(TRADES, outs):
        out[...] = blocks[block_of(here ^ k)]


def gather_pieces(ins, flat):
    here = lax.axis_index("gx")
    for k, piece in zip(TRADES, ins):
        start = 8 * (here ^ k)
        for field in range(flat.shape[0]):
            flat[field, pl.ds(pl.multiple_of(start, 8), 8), :] = piece[field]


def turn_kernel(*refs):
    ins, (own, up, down, flat) = refs[:GROUP], refs[GROUP:]
    gather_pieces(ins, flat)
    for field in range(ADJ):
        for row in range(ROWS):
            own[row, field] = flat[field, pl.ds(row, 8, stride=ROWS), :]
    for table, part in ((FORWARD_UP, up), (FORWARD_DOWN, down)):
        for number, (row, field, _) in enumerate(table):
            if field < ADJ:
                part[number] = own[row, field]
            else:
                group, base = (UPWARD, 2) if row else (DOWNWARD, 0)
                edge, slot = divmod(group.index(field - ADJ), 2)
                part[number] = flat[ADJ + edge, pl.ds(base + slot, 8, stride=ROWS), :]


def turn_adjoint_kernel(*refs):
    ins, (adj, flat) = refs[:GROUP], refs[GROUP:]
    gather_pieces(ins, flat)
    for field in range(Q):
        for row in range(ROWS):
            adj[row, field] = flat[field, pl.ds(row, 8, stride=ROWS), :]


def stream_pull(source, row, sign):
    return [shifted(source[row + 1 - sign * VELOCITIES[i][1], i], i, sign) for i in range(Q)]


def place(target, own_half, packed, number, reach):
    target[:, :128] = own_half
    target[:, 128:] = unpack_strip(packed, number, reach)


def forward_kernel(
    own_a, own_b, adj_a, adj_b, lo_a, lo_b, hi_a, hi_b, lam_ref, sens_ref, mom1, mom2, rs_ref, up, down, p0, p1, p2, a4
):
    def target(field, row):
        if field < Q:
            return p0.at[row + 3, field]
        return rs_ref.at[row + 2, field - RES] if field < ADJ else a4.at[row + 1, field - ADJ]

    for side, own, adj in ((0, own_a, adj_a), (1, own_b, adj_b)):
        lanes = slice(128 * side, 128 * side + 128)
        for row, field in OWN:
            target(field, row)[:, lanes] = own[row, field]
        for row, field in OWN_ADJOINT:
            target(ADJ + field, row)[:, lanes] = adj[row, field]
    for table, parts in ((FORWARD_UP, (lo_a, lo_b)), (FORWARD_DOWN, (hi_a, hi_b))):
        for side, part in enumerate(parts):
            for number, (_, field, row) in enumerate(table):
                target(field, row)[:, slice(128 * side, 128 * side + 128)] = part[number]
    for row in range(ROWS + 4):
        f = stream_pull(p0, row, 1)
        moment = moments(f)
        for j in range(4):
            mom1[row, j] = moment[j]
        out = collide_lists(f, *moment, rs_ref[row, 0], rs_ref[row, 1] == 1.0)
        for i in inward(row, ROWS + 3, 1):
            p1[row, i] = out[i]
    for row in range(ROWS + 2):
        f = stream_pull(p1, row, 1)
        moment = moments(f)
        for j in range(4):
            mom2[row, j] = moment[j]
        out = collide_lists(f, *moment, rs_ref[row + 1, 0], rs_ref[row + 1, 1] == 1.0)
        for i in inward(row, ROWS + 1, 1):
            p2[row, i] = out[i]
    for row in range(ROWS):
        moment = moments(stream_pull(p2, row, 1))
        mu = stream_pull(a4, row, -1)
        out, design = adjoint_lists(mu, *moment, rs_ref[row + 2, 0], rs_ref[row + 2, 1] == 1.0)
        for i in range(Q):
            lam_ref[row, i] = out[i]
        sens_ref[row] = design[:, :128]
    for table, part in ((BACKWARD_UP, up), (BACKWARD_DOWN, down)):
        others = []
        for number, (row, field, _) in enumerate(table):
            source = lam_ref[row, field] if field < Q else mom2[row + 1, field - Q]
            part[number] = source[:, :128]
            others.append(source[:, 128:])
        for number, tile in enumerate(pack_strips(others, BACKWARD_REACH)):
            part[len(table) + number] = tile


def inner_backward_kernel(lam_ref, sens_ref, mom2, rs_ref, l2, sens_out):
    for row in (0, ROWS - 1):
        sens_out[row] = sens_ref[row]
    for row in range(ROWS - 2):
        mu = stream_pull(lam_ref, row, -1)
        moment = [mom2[row + 2, j] for j in range(4)]
        out, design = adjoint_lists(mu, *moment, rs_ref[row + 3, 0], rs_ref[row + 3, 1] == 1.0)
        for i in range(Q):
            l2[row, i] = out[i]
        sens_out[row + 1] = sens_ref[row + 1] + design[:, :128]


def backward_kernel(lam_ref, sens_ref, mom1, mom2, rs_ref, l2_inner, lo, hi, *refs):
    outs, (l3, l2, l1, m2, flat) = refs[:GROUP], refs[GROUP:]
    for row in range(ROWS):
        for i in range(Q):
            l3[row + 3, i] = lam_ref[row, i]
    for row in range(ROWS + 2):
        for j in range(4):
            m2[row + 1, j] = mom2[row, j]
    for table, part in ((BACKWARD_UP, lo), (BACKWARD_DOWN, hi)):
        packed = [part[len(table) + number] for number in range(strip_count(table, BACKWARD_REACH))]
        for number, (_, field, row) in enumerate(table):
            target = l3.at[row + 3, field] if field < Q else m2.at[row + 2, field - Q]
            place(target, part[number], packed, number, BACKWARD_REACH)
    designs = [sens_ref[row] for row in range(ROWS)]
    for row in range(ROWS + 4):
        if 3 <= row < ROWS + 1:
            for i in range(Q):
                l2[row, i] = l2_inner[row - 3, i]
            continue
        mu = stream_pull(l3, row, -1)
        out, design = adjoint_lists(mu, *[m2[row, j] for j in range(4)], rs_ref[row, 0], rs_ref[row, 1] == 1.0)
        for i in inward(row, ROWS + 3, -1):
            l2[row, i] = out[i]
        if 2 <= row < ROWS + 2:
            designs[row - 2] = designs[row - 2] + design[:, :128]
    for row in range(ROWS + 2):
        mu = stream_pull(l2, row, -1)
        moment = [mom1[row + 1, j] for j in range(4)]
        out, design = adjoint_lists(mu, *moment, rs_ref[row + 1, 0], rs_ref[row + 1, 1] == 1.0)
        for i in inward(row, ROWS + 1, -1):
            l1[row, i] = out[i]
        if 1 <= row < ROWS + 1:
            designs[row - 1] = designs[row - 1] + design[:, :128]
    for row in range(ROWS):
        flat[Q, pl.ds(row, 8, stride=ROWS), :] = designs[row]
        mu = stream_pull(l1, row, -1)
        for i in range(Q):
            flat[i, pl.ds(row, 8, stride=ROWS), :] = mu[i][:, :128]
    here = lax.axis_index("gx")
    for k, out in zip(TRADES, outs):
        start = 8 * (here ^ k)
        for i in range(Q + 1):
            out[i] = flat[i, pl.ds(pl.multiple_of(start, 8), 8), :]


def finish_kernel(f_ref, r_ref, s_ref, *refs):
    ins, (lam_ref, sens_ref, blocks) = refs[:GROUP], refs[GROUP:]
    here = lax.axis_index("gx")
    for k, piece in zip(TRADES, ins):
        blocks[block_of(here ^ k)] = piece[...]
    for half in range(2):
        rows = pl.ds(8 * half, 8)
        for layer in range(LAYERS):
            part = slice(4 * layer, 4 * layer + 4)
            tile = [
                jnp.concatenate([blocks[2 * half, i, part, :], blocks[2 * half + 1, i, part, :]], axis=0)
                for i in range(Q + 1)
            ]
            f = [f_ref[i, layer, rows, :] for i in range(Q)]
            out, design = adjoint_lists(tile[:Q], *moments(f), r_ref[layer, rows, :], s_ref[layer, rows, :] == 1)
            for i in range(Q):
                lam_ref[i, layer, rows, :] = out[i]
            sens_ref[layer, rows, :] = tile[Q] + design


def call(kernel, outs, scratch, *args, space=pltpu.VMEM):
    vmem = pl.BlockSpec(memory_space=pltpu.VMEM)
    return pl.pallas_call(
        kernel,
        out_shape=[jax.ShapeDtypeStruct(shape, jnp.float32) for shape in outs],
        in_specs=[pl.BlockSpec(memory_space=space)] * len(args),
        out_specs=[vmem] * len(outs),
        scratch_shapes=[pltpu.VMEM(shape, jnp.float32) if isinstance(shape, tuple) else shape for shape in scratch],
        compiler_params=pltpu.CompilerParams(vmem_limit_bytes=VMEM_LIMIT),
    )(*args)


def ring_pairs(planes, step):
    order = []
    for plane in range(planes):
        for block in range(GROUP):
            gray = (plane - block) % GROUP
            order.append((gray ^ (gray >> 1)) * planes + plane)
    return [(here, order[(at + step) % len(order)]) for at, here in enumerate(order)]


def fast_body(checkpoint, resistance, solid, adjoint_final):
    planes = lax.axis_size("gy")

    def trade(pieces):
        moved = [pieces[0]]
        for number, k in enumerate(TRADES[1:], 1):
            moved.append(lax.ppermute(pieces[number], "gx", [(i, i ^ k) for i in range(GROUP)]))
        return moved

    def swap(value):
        return lax.ppermute(value, "gz", [(0, 1), (1, 0)])

    def ring(up, down):
        lo = lax.ppermute(up, ("gx", "gy"), ring_pairs(planes, 1))
        hi = lax.ppermute(down, ("gx", "gy"), ring_pairs(planes, -1))
        return lo, hi

    given = (checkpoint, resistance, solid, adjoint_final)
    pieces = call(
        send_kernel,
        [(FIELDS, 8, 128)] * GROUP,
        [(GROUP, FIELDS, 8, 128)]
        + [pltpu.VMEM(array.shape, array.dtype) for array in given]
        + [pltpu.SemaphoreType.DMA((len(given),))],
        *[pltpu.with_memory_space_constraint(array, pltpu.HBM) for array in given],
        space=pltpu.HBM,
    )
    fenced = lax.optimization_barrier((adjoint_final, *pieces))
    adjoint_pieces = call(
        send_adjoint_kernel,
        [(Q, 8, 128)] * GROUP,
        [(GROUP, Q, 8, 128), pltpu.VMEM(adjoint_final.shape, jnp.float32), pltpu.SemaphoreType.DMA],
        pltpu.with_memory_space_constraint(fenced[0], pltpu.HBM),
        space=pltpu.HBM,
    )
    pieces = trade(fenced[1:])
    own, up, down = call(
        turn_kernel,
        [(ROWS, ADJ, 8, 128), (len(FORWARD_UP), 8, 128), (len(FORWARD_DOWN), 8, 128)],
        [(FIELDS, 8 * ROWS, 128)],
        *pieces,
    )
    own_b = swap(own)
    (adj,) = call(turn_adjoint_kernel, [(ROWS, Q, 8, 128)], [(Q, 8 * ROWS, 128)], *trade(adjoint_pieces))
    adj_b = swap(adj)
    lo, hi = ring(up, down)
    lo_b, hi_b = swap(lo), swap(hi)
    lam, sens, mom1, mom2, rs, up, down = call(
        forward_kernel,
        [
            (ROWS, Q, 8, 256),
            (ROWS, 8, 128),
            (ROWS + 4, 4, 8, 256),
            (ROWS + 2, 4, 8, 256),
            (ROWS + 4, 2, 8, 256),
            (len(BACKWARD_UP) + strip_count(BACKWARD_UP, BACKWARD_REACH), 8, 128),
            (len(BACKWARD_DOWN) + strip_count(BACKWARD_DOWN, BACKWARD_REACH), 8, 128),
        ],
        [(ROWS + 6, Q, 8, 256), (ROWS + 4, Q, 8, 256), (ROWS + 2, Q, 8, 256), (ROWS + 2, Q, 8, 256)],
        *(own, own_b, adj, adj_b, lo, lo_b, hi, hi_b),
    )
    lo, hi = ring(up, down)
    l2_inner, sens = call(inner_backward_kernel, [(2, Q, 8, 256), (ROWS, 8, 128)], [], lam, sens, mom2, rs)
    pieces = call(
        backward_kernel,
        [(Q + 1, 8, 128)] * GROUP,
        [
            (ROWS + 6, Q, 8, 256),
            (ROWS + 4, Q, 8, 256),
            (ROWS + 2, Q, 8, 256),
            (ROWS + 4, 4, 8, 256),
            (Q + 1, 8 * ROWS, 128),
        ],
        *(lam, sens, mom1, mom2, rs, l2_inner, lo, hi),
    )
    pieces = trade(pieces)
    return tuple(
        call(
            finish_kernel,
            [checkpoint.shape, resistance.shape],
            [(GROUP, Q + 1, 8, 128)],
            checkpoint,
            resistance,
            solid,
            *pieces,
        )
    )


def padded_2(shard, sides, width):
    for axis, dim in sides:
        count, length = (lax.axis_size(axis), shard.shape[dim])
        up = [(i, (i + 1) % count) for i in range(count)]
        down = [(j, i) for i, j in up]
        last = lax.slice_in_dim(shard, length - width, length, axis=dim)
        leading = lax.slice_in_dim(shard, 0, width, axis=dim)
        before = lax.ppermute(last, axis, up)
        after = lax.ppermute(leading, axis, down)
        shard = jnp.concatenate([before, shard, after], axis=dim)
    return shard


def collide(populations, resistance, solid):
    lattice = jnp.array(VELOCITIES, jnp.float32)
    weights = jnp.array(WEIGHTS, jnp.float32).reshape(-1, 1, 1, 1)
    density = jnp.sum(populations, axis=0)
    momentum = jnp.tensordot(lattice, populations, axes=([0], [0]), precision=lax.Precision.HIGHEST)
    nothing = jnp.zeros_like(density)
    push = jnp.stack([BODY_FORCE * density, nothing, nothing]) - resistance[None] * momentum
    velocity = (momentum + RELAXATION * push) / density[None]
    projected = jnp.tensordot(lattice, velocity, axes=([1], [0]), precision=lax.Precision.HIGHEST)
    speed_squared = jnp.sum(velocity * velocity, axis=0)
    equilibrium = (
        weights
        * density[None]
        * (1.0 + 3.0 * projected + 4.5 * projected * projected - 1.5 * speed_squared[None])
    )
    relaxed = populations - (populations - equilibrium) / RELAXATION
    reflected = jnp.stack([populations[other] for other in OPPOSITE])
    return jnp.where(solid[None] == 1, reflected, relaxed)


def transport(field, sign):
    padded = padded_2(field, (("gx", 1), ("gy", 2), ("gz", 3)), 1)
    first, second, third = (field.shape[1], field.shape[2], field.shape[3])
    pieces = []
    for number, entry in enumerate(VELOCITIES):
        start_a = 1 - sign * entry[0]
        start_b = 1 - sign * entry[1]
        start_c = 1 - sign * entry[2]
        pieces.append(
            padded[
                number,
                start_a : start_a + first,
                start_b : start_b + second,
                start_c : start_c + third,
            ]
        )
    return jnp.stack(pieces)


def general_body(checkpoint, resistance, solid, adjoint_final):
    states = [checkpoint]
    current = checkpoint
    for step in range(STEPS - 1):
        current = transport(collide(current, resistance, solid), 1)
        states.append(current)
    adjoint = adjoint_final
    sensitivity = jnp.zeros_like(resistance)
    for step in reversed(range(STEPS)):
        pulled = transport(adjoint, -1)

        def local_collide(populations, design):
            return collide(populations, design, solid)

        result, backward = jax.vjp(local_collide, states[step], resistance)
        adjoint, design_part = backward(pulled)
        sensitivity = sensitivity + design_part
    return (adjoint, sensitivity)


def body(checkpoint, resistance, solid, adjoint_final):
    fits = (
        lax.axis_size("gx") == GROUP
        and lax.axis_size("gz") == 2
        and resistance.shape == (LAYERS, GROUP * ROWS, 128)
    )
    chosen = fast_body if fits else general_body
    return chosen(checkpoint, resistance, solid, adjoint_final)


def solution(mesh):
    in_specs = (
        P(None, "gx", "gy", "gz"),
        P("gx", "gy", "gz"),
        P("gx", "gy", "gz"),
        P(None, "gx", "gy", "gz"),
    )
    out_specs = (P(None, "gx", "gy", "gz"), P("gx", "gy", "gz"))
    return jax.shard_map(body, mesh=mesh, in_specs=in_specs, out_specs=out_specs, check_vma=False)
```
